256 devices in a mesh: hop: 2 (over x_hi), batch: 128 (over y, z, x_lo, core).
Axes of the slice: x: 4 (x_hi: 2, x_lo: 2; x = x_hi * 2 + x_lo), y: 4, z: 8, core: 2. Of those that a mesh axis runs over, the one named last changes fastest.
Arguments:
- section_rows: bfloat16 [2, 16384, 2048], P('hop', 'batch'), may hold values from -6 to 6
- weights: bfloat16 [2, 2048, 2048], P('hop'), may hold values from -0.125 to 0.125
- relation_table: bfloat16 [256, 2048], replicated, may hold values from -4 to 4
- relation_ids: int32 [16384], P('batch'), may hold values from 0 to 255
Outputs:
- weight_grad: float32 [2, 2048, 2048], P('hop', 'batch')
- relation_grad: float32 [256, 2048], P(('hop', 'batch'))
- query_grad: bfloat16 [16384, 2048], P('batch')
The draws below stay inside these ranges and needn't reach their ends.
Inputs may be any that keep to these rules, and one draw needn't show every extreme that they name: `relation_ids`: relation index of each query.
All inputs are finite; a program needn't handle non-finite values.
Results may differ from the reference program's by a relative error of at most 0.0064.
Values may be sent and summed in bfloat16 or wider, within the bound.
A program may use at most 128 MiB of HBM per device.

```python
import jax
import jax.numpy as jnp
from jax import lax

D = 2048
HID = 2048
NREL = 256
TOKENS = 16384


def touch_ends(drawn, stream_key, low, high):
    place = [jax.random.randint(jax.random.fold_in(stream_key, axis), (), 0, length) for axis, length in enumerate(drawn.shape)]
    longest = drawn.shape.index(max(drawn.shape))
    next_to = place[:longest] + [(place[longest] + 1) % drawn.shape[longest]] + place[longest + 1:]
    return drawn.at[tuple(place)].set(low).at[tuple(next_to)].set(high)


def block_scale(stream_key, extent, split, smallest, largest):
    level = 1.0
    for dim, shards_of in split:
        steps = jax.random.uniform(jax.random.fold_in(jax.random.fold_in(stream_key, 6), dim), (shards_of,), jnp.float32, smallest / len(split), largest / len(split))
        level = level * jnp.repeat(jnp.exp(steps), extent[dim] // shards_of).reshape((-1,) + (1,) * (len(extent) - 1 - dim))
    return level


def gaussian(key, extent, spread, reach, shards=(), kind=jnp.bfloat16):
    array = spread * jax.random.normal(key, extent, jnp.float32)
    if shards:
        array = array * block_scale(key, extent, shards, -0.22, 0.18)
    return jnp.clip(array, -reach, reach).astype(kind)


def setup_inputs(seed: int = 0) -> dict:
    key_list = jax.random.split(jax.random.key(seed), 5)
    return {
        "section_rows": gaussian(key_list[0], (2, TOKENS, HID), 1.0, 6.0, ((0, 2), (1, 128))),
        "weights": gaussian(key_list[1], (2, D, HID), D ** -0.5, 0.125, ((0, 2),)),
        "relation_table": gaussian(key_list[2], (NREL, D), 0.7, 4.0),
        "relation_ids": touch_ends(jax.random.randint(key_list[3], (TOKENS,), 0, NREL), jax.random.fold_in(key_list[3], 1), 0, NREL - 1).astype(jnp.int32),
    }


def reference(section_rows, weights, relation_table, relation_ids):
    half = D // 2
    hidden_one = section_rows[0]
    cotangent = section_rows[1]
    query = lax.dot_general(hidden_one, weights[0], (((1,), (1,)), ((), ())), preferred_element_type=jnp.float32).astype(jnp.bfloat16)
    rel = relation_table[relation_ids].astype(jnp.float32)
    r_re = rel[:, :half]
    r_im = rel[:, half:]
    qf = query.astype(jnp.float32)
    q_re = qf[:, :half]
    q_im = qf[:, half:]
    mixed = jnp.concatenate([q_re * r_re - q_im * r_im, q_re * r_im + q_im * r_re], axis=1).astype(jnp.bfloat16)
    pre = jnp.dot(mixed, weights[1], preferred_element_type=jnp.float32)
    sig = jax.nn.sigmoid(pre)
    grad_pre = (cotangent.astype(jnp.float32) * (sig * (1.0 + pre * (1.0 - sig)))).astype(jnp.bfloat16)
    grad_mixed = lax.dot_general(grad_pre, weights[1], (((1,), (1,)), ((), ())), preferred_element_type=jnp.float32)
    gz_re = grad_mixed[:, :half]
    gz_im = grad_mixed[:, half:]
    query_grad = jnp.concatenate([gz_re * r_re + gz_im * r_im, gz_im * r_re - gz_re * r_im], axis=1).astype(jnp.bfloat16)
    grad_rel = jnp.concatenate([gz_re * q_re + gz_im * q_im, gz_im * q_re - gz_re * q_im], axis=1)
    relation_grad = jax.ops.segment_sum(grad_rel, relation_ids, num_segments=NREL) * jnp.sqrt(jnp.float32(NREL) / jnp.float32(TOKENS))
    scale = 1.0 / jnp.sqrt(jnp.float32(TOKENS))
    grad_zero = jnp.dot(query_grad.T, hidden_one, preferred_element_type=jnp.float32) * scale
    grad_one = jnp.dot(mixed.T, grad_pre, preferred_element_type=jnp.float32) * scale
    weight_grad = jnp.stack([grad_zero, grad_one], axis=0)
    return (weight_grad, relation_grad, query_grad)
```

```python
import functools
import math

import jax
import jax.numpy as jnp
from jax import lax
from jax.experimental import pallas as pl
from jax.experimental.pallas import tpu as pltpu
from jax.sharding import PartitionSpec as P

MESH = pl.DeviceIdType.MESH
BF = jnp.bfloat16
F32 = jnp.float32
NY, NZ, NX, NC = 4, 8, 2, 2
CHUNKS = 4
PIECES = 2


def dot(a, b):
    return jnp.dot(a, b, preferred_element_type=F32)


def dot_t(a, b):
    return lax.dot_general(a, b, (((1,), (1,)), ((), ())), preferred_element_type=F32)


def remote(src, dst, send, recv, device):
    return pltpu.make_async_remote_copy(
        src_ref=src, dst_ref=dst, send_sem=send, recv_sem=recv,
        device_id=device, device_id_type=MESH,
    )


def ring(n, index, own, send_far, send_near, recv_far, recv_near, ssem, rsem, devices, finish):
    half = n // 2
    cut = send_far.shape[-1]

    def copy(way, step):
        src = send_far.at[way] if step == 1 else send_near.at[way, step - 2]
        dst = recv_far.at[way] if step == 1 else recv_near.at[way, step - 2]
        return remote(src, dst, ssem.at[way, step - 1], rsem.at[way, step - 1], devices[way])

    def first():
        block = own(lax.rem(index + half, n)).astype(BF)
        send_far[0] = block[:, :cut]
        copy(0, 1).start()
        send_far[1] = block[:, cut:]
        copy(1, 1).start()

    def middle(step):
        distance = half + 1 - step
        for way in (0, 1):
            target = lax.rem(index + (distance if way == 0 else n - distance), n)
            block = own(target)
            copy(way, step - 1).wait_recv()
            if step == 2:
                got = recv_far[way].astype(F32)
                low, high = block[:, :cut], block[:, cut:]
                low, high = (low + got, high) if way == 0 else (low, high + got)
                send_near[way, 0, :, :cut] = low.astype(BF)
                send_near[way, 0, :, cut:] = high.astype(BF)
            else:
                got = recv_near[way, step - 3].astype(F32)
                send_near[way, step - 2] = (block + got).astype(BF)
            copy(way, step).start()

    def last():
        block = own(index)
        copy(0, half).wait_recv()
        copy(1, half).wait_recv()
        finish(block + recv_near[0, half - 2].astype(F32) + recv_near[1, half - 2].astype(F32))

    def drain():
        for step in range(1, half + 1):
            for way in (0, 1):
                copy(way, step).wait_send()

    steps = [first] + [functools.partial(middle, s) for s in range(2, half + 1)] + [last]
    return steps, drain


def kernel(rows_total, rows_ref, w_ref, table_ref, ids_ref, wg_ref, rg_ref, qg_ref, s):
    hop = lax.axis_index("hop")
    place = lax.axis_index("batch")
    core = lax.rem(place, NC)
    x = lax.rem(place // NC, NX)
    z = lax.rem(place // (NC * NX), NZ)
    y = place // (NC * NX * NZ)

    def at(h, yy, zz, xx, cc):
        return (h, ((yy * NZ + zz) * NX + xx) * NC + cc)

    other_core = at(hop, y, z, x, 1 - core)
    other_hop = at(1 - hop, y, z, x, core)
    other_x = at(hop, y, z, 1 - x, core)
    other_hop_x = at(1 - hop, y, z, 1 - x, core)
    y_ways = (at(hop, lax.rem(y + 1, NY), z, x, core), at(hop, lax.rem(y + NY - 1, NY), z, x, core))
    z_ways = (at(hop, y, lax.rem(z + 1, NZ), x, core), at(hop, y, lax.rem(z + NZ - 1, NZ), x, core))

    tokens, width = rows_ref.shape
    half = width // 2
    wide = half // CHUNKS
    rels = table_ref.shape[0]

    def w_copy(j):
        part = pl.ds(j * wide, wide)
        return pltpu.make_async_copy(w_ref.at[part], s["w"].at[part], s["w_sem"].at[j])

    for k in range(CHUNKS):
        w_copy(k).start()
        w_copy(k + CHUNKS).start()

    partners = (other_core, other_hop, other_x, other_hop_x) + y_ways + z_ways
    barrier = pltpu.get_barrier_semaphore()
    for device in partners:
        pl.semaphore_signal(barrier, inc=1, device_id=device, device_id_type=MESH)
    pl.semaphore_wait(barrier, len(partners))

    w, left, right, turned = s["w"], s["left"], s["right"], s["turned"]

    def q_copy(k):
        return remote(s["q_s"].at[k], s["q_r"].at[k], s["hop_sem"].at[0, k], s["hop_sem"].at[1, k], other_hop)

    def g_copy(k):
        return remote(s["g_s"].at[k], s["g_r"].at[k], s["hop_sem"].at[0, k], s["hop_sem"].at[1, k], other_hop)

    def right_copy():
        return remote(
            right.at[pl.ds(0, tokens)], right.at[pl.ds(tokens, tokens)],
            s["right_sem"].at[0], s["right_sem"].at[1], other_core,
        )

    group = wide // (NX * NC * 16)

    def left_copy(k, part):
        first = part * half + k * wide
        yy, z0 = first // (width // NY), first % (width // NY) // (width // NY // NZ)
        return remote(
            turned.at[yy, pl.ds(z0, group), :, 1 - core],
            left.at[yy, pl.ds(z0, group), :, :, pl.ds(tokens, tokens)],
            s["left_sem"].at[0, k, part], s["left_sem"].at[1, k, part], other_core,
        )

    def turn(k, part, values):
        first = part * half + k * wide
        yy, z0 = first // (width // NY), first % (width // NY) // (width // NY // NZ)
        flat = values.T.astype(BF)
        for g in range(group):
            for xx in range(NX):
                for cc in range(NC):
                    at_row = ((g * NX + xx) * NC + cc) * 16
                    turned[yy, z0 + g, xx, cc] = flat[at_row:at_row + 16]
        left_copy(k, part).start()
        left[yy, z0:z0 + group, :, :, 0:tokens] = turned[yy, z0:z0 + group, :, core]

    @pl.when(hop == 0)
    def _():
        right[0:tokens] = rows_ref[...]
        for k in range(CHUNKS):
            for part in range(2):
                w_copy(k + part * CHUNKS).wait()
                weight = w[pl.ds(part * half + k * wide, wide)]
                s["q_s"][k, :, part * wide:(part + 1) * wide] = dot_t(rows_ref[...], weight).astype(BF)
            q_copy(k).start()
        right_copy().start()
        for k in range(CHUNKS):
            g_copy(k).wait_recv()
            for part in range(2):
                chunk = s["g_r"][k, :, part * wide:(part + 1) * wide]
                qg_ref[:, part * half + k * wide:part * half + (k + 1) * wide] = chunk
                turn(k, part, chunk.astype(F32))
        for k in range(CHUNKS):
            q_copy(k).wait_send()

    @pl.when(hop == 1)
    def _():
        ids = ids_ref[...]
        rows_of = lax.broadcasted_iota(jnp.int32, (rels, tokens), 0)
        onehot = jnp.where(rows_of == ids, 1.0, 0.0).T.astype(BF)
        for n in range(CHUNKS):
            part = slice(n * 2 * wide, (n + 1) * 2 * wide)
            s["rel"][:, part] = dot(onehot, table_ref[:, part]).astype(BF)
        for k in range(CHUNKS):
            re = slice(k * wide, (k + 1) * wide)
            im = slice(half + k * wide, half + (k + 1) * wide)
            w_copy(k).wait()
            w_copy(k + CHUNKS).wait()
            r_re, r_im = s["rel"][:, re].astype(F32), s["rel"][:, im].astype(F32)
            q_copy(k).wait_recv()
            q_re = s["q_r"][k, :, :wide].astype(F32)
            q_im = s["q_r"][k, :, wide:].astype(F32)
            z_re = (q_re * r_re - q_im * r_im).astype(BF)
            z_im = (q_re * r_im + q_im * r_re).astype(BF)
            for n in range(CHUNKS):
                part = slice(n * 2 * wide, (n + 1) * 2 * wide)
                term = dot(z_re, w[re, part]) + dot(z_im, w[im, part])
                s["pre"][:, part] = term if k == 0 else s["pre"][:, part] + term
            turn(k, 0, z_re.astype(F32))
            turn(k, 1, z_im.astype(F32))
        for n in range(CHUNKS):
            part = slice(n * 2 * wide, (n + 1) * 2 * wide)
            pre = s["pre"][:, part]
            sig = 1.0 / (1.0 + jnp.exp(-pre))
            slope = sig * (1.0 + pre * (1.0 - sig))
            right[0:tokens, part] = (rows_ref[:, part].astype(F32) * slope).astype(BF)
        right_copy().start()
        for k in range(CHUNKS):
            re = slice(k * wide, (k + 1) * wide)
            im = slice(half + k * wide, half + (k + 1) * wide)
            g_a = right[0:tokens]
            gz_re = dot_t(g_a, w[re])
            gz_im = dot_t(g_a, w[im])
            r_re, r_im = s["rel"][:, re].astype(F32), s["rel"][:, im].astype(F32)
            gq_re = (gz_re * r_re + gz_im * r_im).astype(BF)
            gq_im = (gz_im * r_re - gz_re * r_im).astype(BF)
            s["g_s"][k, :, :wide] = gq_re
            s["g_s"][k, :, wide:] = gq_im
            g_copy(k).start()
            qg_ref[:, re] = gq_re
            qg_ref[:, im] = gq_im
            q_re = s["q_r"][k, :, :wide].astype(F32)
            q_im = s["q_r"][k, :, wide:].astype(F32)
            s["pre"][:, re] = gz_re * q_re + gz_im * q_im
            s["pre"][:, im] = gz_im * q_re - gz_re * q_im

        line = lax.broadcasted_iota(jnp.int32, (rels, tokens), 0)
        yz, rest = line // 8, lax.rem(line, 8)
        col_half = rest // 4
        base = lax.rem(rest // 2, 2) * (rels // 2) + yz * (NX * NC) + lax.rem(rest, 2) * NC

        def partial_for(which):
            match = jnp.where(base + which == ids, 1.0, 0.0)
            total = None
            for side in range(2):
                pick = jnp.where(col_half == side, match, 0.0).astype(BF)
                values = s["pre"][:, side * half:(side + 1) * half]
                head = values.astype(BF)
                tail = (values - head.astype(F32)).astype(BF)
                term = dot(pick, head) + dot(pick, tail)
                total = term if total is None else total + term
            return total.reshape(NY, NZ, 8, half)

        swap = remote(s["rp_s"], s["rp_r"], s["rel_sem"].at[0, 4], s["rel_sem"].at[1, 4], other_core)
        s["rp_s"][...] = partial_for(1 - core).astype(BF)
        swap.start()
        s["rp"][...] = partial_for(core)
        swap.wait()
        s["rp"][...] = s["rp"][...] + s["rp_r"][...].astype(F32)
        for k in range(CHUNKS):
            g_copy(k).wait_send()

    for k in range(CHUNKS):
        for part in range(2):
            left_copy(k, part).wait()
    right_copy().wait()

    colour = width // 2
    piece = colour // PIECES

    def product_z(p):
        def own(zz):
            a = left[:, zz].reshape(NY * NX * 16, 2 * tokens)
            return dot(a, right[:, p * piece:(p + 1) * piece])
        return own

    def product_y(p):
        def own(yy):
            a = left[yy].reshape(NZ * NX * 16, 2 * tokens)
            return dot(a, right[:, colour + p * piece:colour + (p + 1) * piece])
        return own

    events = []
    drains = []
    seq = [0]

    def chain(times, first, second, guard):
        (steps_a, drain_a), (steps_b, drain_b) = first, second
        for t, step in zip(times, steps_a + steps_b):
            seq[0] += 1
            events.append((t, seq[0], guard, step))
        drains.append((guard, drain_a))
        drains.append((guard, drain_b))

    z_times = [0, 4, 10, 16, 22, 22.5, 26, 29]
    y_times = [0, 7, 19, 19.5, 22.2, 25, 28, 30]

    def bufs(name):
        return [s[name + "_" + b] for b in ("sf", "sn", "rf", "rn", "ss", "rs")]

    def sub(refs, p):
        return [r.at[p] for r in refs]

    for p in range(PIECES):
        cols = slice(p * piece, (p + 1) * piece)

        def keep_z(v, cols=cols):
            s["sum_z"][:, :, cols] = v.reshape(NY, NX * 16, piece)

        def keep_y(v, cols=cols):
            s["sum_y"][:, :, cols] = v.reshape(NZ, NX * 16, piece)

        def end_z(v, cols=cols):
            s["total"][:, :, cols] = v.reshape(NX, 16, piece)

        def end_y(v, p=p):
            s["total"][:, :, colour + p * piece:colour + (p + 1) * piece] = v.reshape(NX, 16, piece)

        def from_z(yy, cols=cols):
            return s["sum_z"][yy, :, cols]

        def from_y(zz, cols=cols):
            return s["sum_y"][zz, :, cols]

        shift = 0.5 * p
        chain(
            [t + shift for t in z_times],
            ring(NZ, z, product_z(p), *sub(bufs("az"), p), z_ways, keep_z),
            ring(NY, y, from_z, *sub(bufs("ay"), p), y_ways, end_z),
            False,
        )
        chain(
            [t + shift + 0.25 for t in y_times],
            ring(NY, y, product_y(p), *sub(bufs("by"), p), y_ways, keep_y),
            ring(NZ, z, from_y, *sub(bufs("bz"), p), z_ways, end_y),
            False,
        )

    rcut = half // 2
    def rel_z(zz):
        return s["rp"][:, zz, :, :rcut].reshape(NY * 8, rcut)

    def rel_y(yy):
        return s["rp"][yy, :, :, rcut:].reshape(NZ * 8, rcut)

    def rkeep_z(v):
        s["rsum_z"][...] = v.reshape(NY, 8, rcut)

    def rkeep_y(v):
        s["rsum_y"][...] = v.reshape(NZ, 8, rcut)

    def rend_z(v):
        s["rtotal"][:, :rcut] = v

    def rend_y(v):
        s["rtotal"][:, rcut:] = v

    chain(
        [t + 0.8 for t in z_times],
        ring(NZ, z, rel_z, *bufs("raz"), z_ways, rkeep_z),
        ring(NY, y, lambda yy: s["rsum_z"][yy], *bufs("ray"), y_ways, rend_z),
        True,
    )
    chain(
        [t + 0.9 for t in y_times],
        ring(NY, y, rel_y, *bufs("rby"), y_ways, rkeep_y),
        ring(NZ, z, lambda zz: s["rsum_y"][zz], *bufs("rbz"), z_ways, rend_y),
        True,
    )

    for _, _, guard, step in sorted(events, key=lambda e: e[:2]):
        if guard:
            pl.when(hop == 1)(step)
        else:
            step()

    x_copy = remote(s["x_s"], s["x_r"], s["x_sem"].at[0], s["x_sem"].at[1], other_x)
    s["x_s"][...] = s["total"][1 - x].astype(BF)
    x_copy.start()

    def rel_out(h, xx, slot, sem, device):
        return remote(
            s["rel_s"].at[h * NX + xx], s["rel_r"].at[slot],
            s["rel_sem"].at[0, sem], s["rel_sem"].at[1, sem], device,
        )

    @pl.when(hop == 1)
    def _():
        v = s["rtotal"][...]
        for h in range(2):
            for xx in range(NX):
                for side in range(2):
                    line = side * 4 + h * 2 + xx
                    s["rel_s"][h * NX + xx, side:side + 1] = v[line:line + 1]
        rel_out(0, x, x, 0, other_hop).start()
        rel_out(0, 1 - x, x, 1, other_hop_x).start()
        rel_out(1, 1 - x, x, 2, other_x).start()

    scale = 1.0 / math.sqrt(rows_total)
    x_copy.wait()
    wg_ref[...] = (s["total"][x] + s["x_r"][...].astype(F32)) * scale
    rel_scale = math.sqrt(rels / rows_total)

    def finish_rel(total):
        rg_ref[:, :half] = total[0:1] * rel_scale
        rg_ref[:, half:] = total[1:2] * rel_scale

    @pl.when(hop == 1)
    def _():
        rel_out(1, 1 - x, 1 - x, 2, other_x).wait_recv()
        finish_rel(s["rel_s"][NX + x] + s["rel_r"][1 - x])
        rel_out(0, x, x, 0, other_hop).wait_send()
        rel_out(0, 1 - x, x, 1, other_hop_x).wait_send()
        rel_out(1, 1 - x, x, 2, other_x).wait_send()

    @pl.when(hop == 0)
    def _():
        rel_out(0, x, x, 0, other_hop).wait_recv()
        rel_out(0, 1 - x, 1 - x, 1, other_hop_x).wait_recv()
        finish_rel(s["rel_r"][0] + s["rel_r"][1])

    for guard, drain in drains:
        if guard:
            pl.when(hop == 1)(drain)
        else:
            drain()


def local(section_rows, weights, relation_table, relation_ids):
    tokens, width = section_rows.shape[1:]
    rels = relation_table.shape[0]
    total = tokens * lax.axis_size("batch")
    half = width // 2
    wide = half // CHUNKS
    piece = width // 2 // PIECES
    V = pltpu.VMEM
    D = pltpu.SemaphoreType.DMA

    scratch = {
        "w": V((width, width), BF),
        "w_sem": D((2 * CHUNKS,)),
        "hop_sem": D((2, CHUNKS)),
        "right_sem": D((2,)),
        "left_sem": D((2, CHUNKS, 2)),
        "rel_sem": D((2, 5)),
        "x_sem": D((2,)),
        "q_s": V((CHUNKS, tokens, 2 * wide), BF),
        "q_r": V((CHUNKS, tokens, 2 * wide), BF),
        "g_s": V((CHUNKS, tokens, 2 * wide), BF),
        "g_r": V((CHUNKS, tokens, 2 * wide), BF),
        "rel": V((tokens, width), BF),
        "pre": V((tokens, width), F32),
        "turned": V((NY, NZ, NX, NC, 16, tokens), BF),
        "left": V((NY, NZ, NX, 16, 2 * tokens), BF),
        "right": V((2 * tokens, width), BF),
        "rp": V((NY, NZ, 8, half), F32),
        "rp_s": V((NY, NZ, 8, half), BF),
        "rp_r": V((NY, NZ, 8, half), BF),
        "sum_z": V((NY, NX * 16, half), F32),
        "sum_y": V((NZ, NX * 16, half), F32),
        "total": V((NX, 16, width), F32),
        "rsum_z": V((NY, 8, half // 2), F32),
        "rsum_y": V((NZ, 8, half // 2), F32),
        "rtotal": V((8, half), F32),
        "x_s": V((16, width), BF),
        "x_r": V((16, width), BF),
        "rel_s": V((2 * NX, 2, half), F32),
        "rel_r": V((NX, 2, half), F32),
    }

    def ring_bufs(name, lead, n, rows, cols):
        h = n // 2
        scratch[name + "_sf"] = V(lead + (2, rows, cols // 2), BF)
        scratch[name + "_sn"] = V(lead + (2, h - 1, rows, cols), BF)
        scratch[name + "_rf"] = V(lead + (2, rows, cols // 2), BF)
        scratch[name + "_rn"] = V(lead + (2, h - 1, rows, cols), BF)
        scratch[name + "_ss"] = D(lead + (2, h))
        scratch[name + "_rs"] = D(lead + (2, h))

    ring_bufs("az", (PIECES,), NZ, NY * NX * 16, piece)
    ring_bufs("ay", (PIECES,), NY, NX * 16, piece)
    ring_bufs("by", (PIECES,), NY, NZ * NX * 16, piece)
    ring_bufs("bz", (PIECES,), NZ, NX * 16, piece)
    ring_bufs("raz", (), NZ, NY * 8, half // 2)
    ring_bufs("ray", (), NY, 8, half // 2)
    ring_bufs("rby", (), NY, NZ * 8, half // 2)
    ring_bufs("rbz", (), NZ, 8, half // 2)
    names = list(scratch)

    def body(*refs):
        kernel(total, *refs[:7], dict(zip(names, refs[7:])))

    vmem = pl.BlockSpec(memory_space=pltpu.VMEM)
    wg, rg, qg = pl.pallas_call(
        body,
        out_shape=(
            jax.ShapeDtypeStruct((16, width), F32),
            jax.ShapeDtypeStruct((1, width), F32),
            jax.ShapeDtypeStruct((tokens, width), BF),
        ),
        in_specs=[vmem, pl.BlockSpec(memory_space=pl.ANY), vmem, vmem],
        out_specs=(vmem, vmem, vmem),
        scratch_shapes=[scratch[n] for n in names],
        compiler_params=pltpu.CompilerParams(
            collective_id=0, has_side_effects=True, vmem_limit_bytes=60 * 1024 * 1024
        ),
        name="backward",
    )(section_rows[0], weights[0], relation_table, relation_ids.reshape(1, tokens))
    return (wg[None], rg, qg)


def solution(mesh):
    return jax.shard_map(
        local,
        mesh=mesh,
        in_specs=(P("hop", "batch", None), P("hop", None, None), P(), P("batch")),
        out_specs=(P("hop", "batch", None), P(("hop", "batch"), None), P("batch", None)),
        check_vma=False,
    )
```

```python
import functools
import math

import jax
import jax.numpy as jnp
from jax import lax
from jax.experimental import pallas as pl
from jax.experimental.pallas import tpu as pltpu
from jax.sharding import PartitionSpec as P

MESH = pl.DeviceIdType.MESH
BF = jnp.bfloat16
F32 = jnp.float32
NY, NZ, NX, NC = 4, 8, 2, 2
CHUNKS = 4
PIECES = 2
BLOCKS = 2


def dot(a, b):
    return jnp.dot(a, b, preferred_element_type=F32)


def dot_t(a, b):
    return lax.dot_general(a, b, (((1,), (1,)), ((), ())), preferred_element_type=F32)


def remote(src, dst, send, recv, device):
    return pltpu.make_async_remote_copy(
        src_ref=src, dst_ref=dst, send_sem=send, recv_sem=recv,
        device_id=device, device_id_type=MESH,
    )


def ring(n, index, own, send_far, send_near, recv_far, recv_near, ssem, rsem, devices, finish):
    half = n // 2
    cut = send_far.shape[-1]

    def copy(way, step):
        src = send_far.at[way] if step == 1 else send_near.at[way, step - 2]
        dst = recv_far.at[way] if step == 1 else recv_near.at[way, step - 2]
        return remote(src, dst, ssem.at[way, step - 1], rsem.at[way, step - 1], devices[way])

    def first():
        block = own(lax.rem(index + half, n)).astype(BF)
        send_far[0] = block[:, :cut]
        copy(0, 1).start()
        send_far[1] = block[:, cut:]
        copy(1, 1).start()

    def middle(step):
        distance = half + 1 - step
        for way in (0, 1):
            target = lax.rem(index + (distance if way == 0 else n - distance), n)
            block = own(target)
            copy(way, step - 1).wait_recv()
            if step == 2:
                got = recv_far[way].astype(F32)
                low, high = block[:, :cut], block[:, cut:]
                low, high = (low + got, high) if way == 0 else (low, high + got)
                send_near[way, 0, :, :cut] = low.astype(BF)
                send_near[way, 0, :, cut:] = high.astype(BF)
            else:
                got = recv_near[way, step - 3].astype(F32)
                send_near[way, step - 2] = (block + got).astype(BF)
            copy(way, step).start()

    def last():
        block = own(index)
        copy(0, half).wait_recv()
        copy(1, half).wait_recv()
        finish(block + recv_near[0, half - 2].astype(F32) + recv_near[1, half - 2].astype(F32))

    def drain():
        for step in range(1, half + 1):
            for way in (0, 1):
                copy(way, step).wait_send()

    steps = [first] + [functools.partial(middle, s) for s in range(2, half + 1)] + [last]
    return steps, drain


def kernel(rows_total, rows_ref, w_ref, table_ref, ids_ref, wg_ref, rg_ref, qg_ref, s):
    hop = lax.axis_index("hop")
    place = lax.axis_index("batch")
    core = lax.rem(place, NC)
    x = lax.rem(place // NC, NX)
    z = lax.rem(place // (NC * NX), NZ)
    y = place // (NC * NX * NZ)

    def at(h, yy, zz, xx, cc):
        return (h, ((yy * NZ + zz) * NX + xx) * NC + cc)

    other_core = at(hop, y, z, x, 1 - core)
    other_hop = at(1 - hop, y, z, x, core)
    other_x = at(hop, y, z, 1 - x, core)
    diagonal = at(hop, y, z, 1 - x, 1 - core)
    across = at(1 - hop, y, z, 1 - x, core)
    y_ways = (at(hop, lax.rem(y + 1, NY), z, x, core), at(hop, lax.rem(y + NY - 1, NY), z, x, core))
    z_ways = (at(hop, y, lax.rem(z + 1, NZ), x, core), at(hop, y, lax.rem(z + NZ - 1, NZ), x, core))

    tokens, width = rows_ref.shape
    block = tokens // BLOCKS
    half = width // 2
    wide = half // CHUNKS
    rels = table_ref.shape[0]
    colour = width // 2
    piece = colour // PIECES
    group = NZ * (NY // 2) // CHUNKS

    def w_copy(j):
        part = pl.ds(j * wide, wide)
        return pltpu.make_async_copy(w_ref.at[part], s["w"].at[part], s["w_sem"].at[j])

    table_copy = pltpu.make_async_copy(table_ref, s["table"], s["table_sem"])
    for k in range(CHUNKS):
        w_copy(k).start()
        w_copy(k + CHUNKS).start()
    table_copy.start()

    partners = (other_core, other_hop, other_x, diagonal, across) + y_ways + z_ways
    barrier = pltpu.get_barrier_semaphore()
    for device in partners:
        pl.semaphore_signal(barrier, inc=1, device_id=device, device_id_type=MESH)
    pl.semaphore_wait(barrier, len(partners))

    w, turned = s["w"], s["turned"]

    def hop_copy(src, dst, b, k):
        return remote(s[src].at[b, k], s[dst].at[b, k], s["hop_sem"].at[0, b, k], s["hop_sem"].at[1, b, k], across)

    def q_copy(b, k):
        return hop_copy("q_s", "q_r", b, k)

    def g_copy(b, k):
        return hop_copy("g_s", "g_r", b, k)

    def spot(k):
        return k // (CHUNKS // 2), k % (CHUNKS // 2) * group

    def turn(k, re, im):
        low, z0 = spot(k)
        for part, values in enumerate((re, im)):
            flat = values.astype(F32).T.astype(BF)
            for g in range(group):
                for xx in range(NX):
                    for cc in range(NC):
                        row = ((g * NX + xx) * NC + cc) * 16
                        turned[part, low, z0 + g, xx, cc] = flat[row:row + 16]

    def bufs(name):
        return [s[name + "_" + b] for b in ("sf", "sn", "rf", "rn", "ss", "rs")]

    def sub(refs, p):
        return [r.at[p] for r in refs]

    def chain(events, times, first, second):
        for t, step in zip(times, first[0] + second[0]):
            events.append((t, len(events), step))

    def run(events):
        for _, _, step in sorted(events, key=lambda e: e[:2]):
            step()

    def weight_rings(name, left, right, rows, events, drains, z_times, y_times, lag):
        depth = right.shape[0]

        def by_z(p):
            def own(zz):
                a = left[:, :, zz].reshape(NY * rows, depth)
                return dot(a, right[:, p * piece:(p + 1) * piece])
            return own

        def by_y(p):
            def own(yy):
                a = left[yy // 2, lax.rem(yy, 2)].reshape(NZ * rows, depth)
                return dot(a, right[:, colour + p * piece:colour + (p + 1) * piece])
            return own

        for p in range(PIECES):
            cols = slice(p * piece, (p + 1) * piece)
            late = slice(colour + p * piece, colour + (p + 1) * piece)

            def keep_z(v, cols=cols):
                s[name + "_sum_z"][:, :, cols] = v.reshape(NY, rows, piece)

            def keep_y(v, cols=cols):
                s[name + "_sum_y"][:, :, cols] = v.reshape(NZ, rows, piece)

            def end_z(v, cols=cols):
                s[name + "_total"][:, cols] = v

            def end_y(v, late=late):
                s[name + "_total"][:, late] = v

            def from_z(yy, cols=cols):
                return s[name + "_sum_z"][yy, :, cols]

            def from_y(zz, cols=cols):
                return s[name + "_sum_y"][zz, :, cols]

            one = ring(NZ, z, by_z(p), *sub(bufs(name + "_az"), p), z_ways, keep_z)
            two = ring(NY, y, from_z, *sub(bufs(name + "_ay"), p), y_ways, end_z)
            chain(events, [t + lag * p for t in z_times], one, two)
            three = ring(NY, y, by_y(p), *sub(bufs(name + "_by"), p), y_ways, keep_y)
            four = ring(NZ, z, from_y, *sub(bufs(name + "_bz"), p), z_ways, end_y)
            chain(events, [t + lag * p + lag / 2 for t in y_times], three, four)
            drains += [one[1], two[1], three[1], four[1]]

    scale = 1.0 / math.sqrt(rows_total)
    rel_scale = math.sqrt(rels / rows_total)

    def rel_out(h, xx, slot, sem, device):
        return remote(
            s["rel_s"].at[h * NX + xx], s["rel_r"].at[slot],
            s["rel_sem"].at[0, sem], s["rel_sem"].at[1, sem], device,
        )

    def finish_rel(total):
        rg_ref[:, :half] = total[0:1] * rel_scale
        rg_ref[:, half:] = total[1:2] * rel_scale

    @pl.when(hop == 0)
    def _():
        left, right = s["left0"], s["right0"]
        dest = (None, other_core, other_x, diagonal)

        def slot(n):
            return right.at[pl.ds(n * tokens, tokens)]

        sends = s["right0_sem"]
        to_core = remote(rows_ref, slot(1), sends.at[0, 0], sends.at[1, 0], other_core)
        to_x = remote(rows_ref, slot(2), sends.at[0, 1], sends.at[1, 1], other_x)
        onward = remote(slot(2), slot(3), sends.at[0, 2], sends.at[1, 2], other_core)
        to_x.start()

        for k in range(CHUNKS):
            for part in range(2):
                w_copy(k + part * CHUNKS).wait()
                weight = w[pl.ds(part * half + k * wide, wide)]
                q = dot_t(rows_ref[...], weight).astype(BF)
                for b in range(BLOCKS):
                    s["q_s"][b, k, :, part * wide:(part + 1) * wide] = q[b * block:(b + 1) * block]
            q_copy(0, k).start()
        for b in range(1, BLOCKS):
            for k in range(CHUNKS):
                q_copy(b, k).start()
        to_core.start()
        right[0:tokens] = rows_ref[...]
        table_copy.wait()

        def left_copy(k, n):
            low, z0 = spot(k)
            xx, cc = (x, 1 - core) if n == 1 else (1 - x, core if n == 2 else 1 - core)
            return remote(
                turned.at[:, low, pl.ds(z0, group), xx, cc],
                left.at[:, low, pl.ds(z0, group), :, pl.ds(n * tokens, tokens)],
                s["left0_sem"].at[0, k, n - 1], s["left0_sem"].at[1, k, n - 1], dest[n],
            )

        for b in range(BLOCKS):
            line = slice(b * block, (b + 1) * block)
            for k in range(CHUNKS):
                re = slice(k * wide, (k + 1) * wide)
                im = slice(half + k * wide, half + (k + 1) * wide)
                g_copy(b, k).wait_recv()
                qg_ref[line, re] = s["g_r"][b, k, :, :wide]
                qg_ref[line, im] = s["g_r"][b, k, :, wide:]
                if b == BLOCKS - 1:
                    low, z0 = spot(k)
                    turn(k, qg_ref[:, re], qg_ref[:, im])
                    for n in (2, 3, 1):
                        left_copy(k, n).start()
                    left[:, low, z0:z0 + group, :, 0:tokens] = turned[:, low, z0:z0 + group, x, core]
            if b == 0:
                to_x.wait_recv()
                onward.start()
        to_core.wait()
        to_x.wait_send()
        onward.wait()
        for k in range(CHUNKS):
            for n in (1, 2, 3):
                left_copy(k, n).wait()

        events, drains = [], []
        weight_rings(
            "h0", left, right, 16, events, drains,
            [0, 3, 6.5, 10, 13.5, 14, 17, 20], [0, 4, 10.5, 11, 13, 15.5, 18, 20.5], 0.5,
        )
        run(events)
        wg_ref[...] = s["h0_total"][...] * scale
        for b in range(BLOCKS):
            for k in range(CHUNKS):
                q_copy(b, k).wait_send()
        for drain in drains:
            drain()
        rel_out(0, x, x, 0, other_hop).wait_recv()
        rel_out(0, 1 - x, 1 - x, 1, across).wait_recv()
        finish_rel(s["rel_r"][0] + s["rel_r"][1])

    @pl.when(hop == 1)
    def _():
        left, right = s["left1"], s["right1"]

        def cot_copy(b):
            line = pl.ds(b * block, block)
            return remote(rows_ref.at[line], s["cot"].at[line], s["cot_sem"].at[0, b], s["cot_sem"].at[1, b], other_x)

        def out_copy(b, k):
            return remote(s["g_s"].at[b, k], s["o_r"].at[b, k], s["out_sem"].at[0, b, k], s["out_sem"].at[1, b, k], other_x)

        def right_copy(b):
            return remote(
                right.at[pl.ds(b * block, block)], right.at[pl.ds(tokens + b * block, block)],
                s["right1_sem"].at[0, b], s["right1_sem"].at[1, b], other_core,
            )

        def left_copy(k):
            low, z0 = spot(k)
            return remote(
                turned.at[:, low, pl.ds(z0, group), :, 1 - core],
                left.at[:, low, pl.ds(z0, group), :, :, pl.ds(tokens, tokens)],
                s["left1_sem"].at[0, k], s["left1_sem"].at[1, k], other_core,
            )

        ids_copy = remote(ids_ref, s["ids"], s["ids_sem"].at[0], s["ids_sem"].at[1], other_x)
        ids_copy.start()
        for b in range(BLOCKS):
            cot_copy(b).start()
        ids_copy.wait()
        ids = s["ids"][...]
        rows_of = lax.broadcasted_iota(jnp.int32, (rels, tokens), 0)
        onehot = jnp.where(rows_of == ids, 1.0, 0.0).T.astype(BF)
        table_copy.wait()
        for n in range(CHUNKS):
            part = slice(n * 2 * wide, (n + 1) * 2 * wide)
            s["rel"][:, part] = dot(onehot, s["table"][:, part]).astype(BF)
        for k in range(CHUNKS):
            w_copy(k).wait()
            w_copy(k + CHUNKS).wait()

        def columns(k):
            return slice(k * wide, (k + 1) * wide), slice(half + k * wide, half + (k + 1) * wide)

        def forward(b, k):
            re, im = columns(k)
            line = slice(b * block, (b + 1) * block)
            r_re, r_im = s["rel"][line, re].astype(F32), s["rel"][line, im].astype(F32)
            q_copy(b, k).wait_recv()
            q_re = s["q_r"][b, k, :, :wide].astype(F32)
            q_im = s["q_r"][b, k, :, wide:].astype(F32)
            z_re = (q_re * r_re - q_im * r_im).astype(BF)
            z_im = (q_re * r_im + q_im * r_re).astype(BF)
            s["mixed"][line, re] = z_re
            s["mixed"][line, im] = z_im
            for n in range(CHUNKS):
                part = slice(n * 2 * wide, (n + 1) * 2 * wide)
                term = dot(z_re, w[re, part]) + dot(z_im, w[im, part])
                s["pre"][line, part] = term if k == 0 else s["pre"][line, part] + term

        def activate(b):
            line = slice(b * block, (b + 1) * block)
            cot_copy(b).wait_recv()
            for n in range(CHUNKS):
                part = slice(n * 2 * wide, (n + 1) * 2 * wide)
                pre = s["pre"][line, part]
                sig = 1.0 / (1.0 + jnp.exp(-pre))
                slope = sig * (1.0 + pre * (1.0 - sig))
                right[line, part] = (s["cot"][line, part].astype(F32) * slope).astype(BF)
            right_copy(b).start()

        def back(b, k):
            re, im = columns(k)
            line = slice(b * block, (b + 1) * block)
            g_a = right[line]
            gz_re = dot_t(g_a, w[re])
            gz_im = dot_t(g_a, w[im])
            r_re, r_im = s["rel"][line, re].astype(F32), s["rel"][line, im].astype(F32)
            s["g_s"][b, k, :, :wide] = (gz_re * r_re + gz_im * r_im).astype(BF)
            s["g_s"][b, k, :, wide:] = (gz_im * r_re - gz_re * r_im).astype(BF)
            g_copy(b, k).start()
            out_copy(b, k).start()
            q_re = s["q_r"][b, k, :, :wide].astype(F32)
            q_im = s["q_r"][b, k, :, wide:].astype(F32)
            s["pre"][line, re] = gz_re * q_re + gz_im * q_im
            s["pre"][line, im] = gz_im * q_re - gz_re * q_im

        for b in range(BLOCKS):
            for k in range(CHUNKS):
                forward(b, k)
            activate(b)
            for k in range(CHUNKS):
                back(b, k)
        for k in range(CHUNKS):
            re, im = columns(k)
            low, z0 = spot(k)
            turn(k, s["mixed"][:, re], s["mixed"][:, im])
            left_copy(k).start()
            left[:, low, z0:z0 + group, :, :, 0:tokens] = turned[:, low, z0:z0 + group, :, core]
        for b in range(BLOCKS):
            right_copy(b).wait()
        for k in range(CHUNKS):
            left_copy(k).wait()

        swap = remote(s["rp_s"], s["rp_r"], s["rel_sem"].at[0, 3], s["rel_sem"].at[1, 3], other_core)

        def rel_start():
            row = lax.broadcasted_iota(jnp.int32, (rels, tokens), 0)
            yz, rest = row // 8, lax.rem(row, 8)
            col_half = rest // 4
            base = lax.rem(rest // 2, 2) * (rels // 2) + yz * (NX * NC) + lax.rem(rest, 2) * NC
            who = s["ids"][...]

            def partial_for(which):
                match = jnp.where(base + which == who, 1.0, 0.0)
                total = None
                for side in range(2):
                    pick = jnp.where(col_half == side, match, 0.0).astype(BF)
                    values = s["pre"][:, side * half:(side + 1) * half]
                    head = values.astype(BF)
                    tail = (values - head.astype(F32)).astype(BF)
                    term = dot(pick, head) + dot(pick, tail)
                    total = term if total is None else total + term
                return total.reshape(NY, NZ, 8, half)

            s["rp_s"][...] = partial_for(1 - core).astype(BF)
            swap.start()
            s["rp"][...] = partial_for(core)

        def rel_join():
            swap.wait()
            s["rp"][...] = s["rp"][...] + s["rp_r"][...].astype(F32)

        cut = half // 2

        def rkeep_z(v):
            s["rsum_z"][...] = v.reshape(NY, 8, cut)

        def rkeep_y(v):
            s["rsum_y"][...] = v.reshape(NZ, 8, cut)

        def rend_z(v):
            s["rtotal"][:, :cut] = v

        def rend_y(v):
            s["rtotal"][:, cut:] = v

        def rel_z(zz):
            return s["rp"][:, zz, :, :cut].reshape(NY * 8, cut)

        def rel_y(yy):
            return s["rp"][yy, :, :, cut:].reshape(NZ * 8, cut)

        events, drains = [], []
        z_times = [0, 4, 10, 16, 22, 22.5, 26, 29]
        y_times = [0, 7, 19, 19.5, 22.2, 25, 28, 30]
        weight_rings("h1", left, right, NX * 16, events, drains, z_times, y_times, 0.5)
        events += [(1.5, 900, rel_start), (3.9, 901, rel_join)]
        one = ring(NZ, z, rel_z, *bufs("raz"), z_ways, rkeep_z)
        two = ring(NY, y, lambda yy: s["rsum_z"][yy], *bufs("ray"), y_ways, rend_z)
        chain(events, [3.95, 8.8, 11, 16.8, 22.8, 22.85, 26.8, 29.8], one, two)
        three = ring(NY, y, rel_y, *bufs("rby"), y_ways, rkeep_y)
        four = ring(NZ, z, lambda zz: s["rsum_y"][zz], *bufs("rbz"), z_ways, rend_y)
        chain(events, [3.96, 8.9, 19.9, 19.95, 22.9, 25.9, 28.9, 30.9], three, four)
        drains += [one[1], two[1], three[1], four[1]]
        run(events)

        total = s["h1_total"]
        x_copy = remote(s["x_s"], s["x_r"], s["x_sem"].at[0], s["x_sem"].at[1], other_x)
        s["x_s"][...] = total[pl.ds(pl.multiple_of((1 - x) * 16, 16), 16)].astype(BF)
        x_copy.start()

        v = s["rtotal"][...]
        for h in range(2):
            for xx in range(NX):
                for side in range(2):
                    row = side * 4 + h * 2 + xx
                    s["rel_s"][h * NX + xx, side:side + 1] = v[row:row + 1]
        outs = (
            rel_out(0, x, x, 0, other_hop),
            rel_out(0, 1 - x, x, 1, across),
            rel_out(1, 1 - x, x, 2, other_x),
        )
        for out in outs:
            out.start()
        for b in range(BLOCKS):
            line = slice(b * block, (b + 1) * block)
            for k in range(CHUNKS):
                re, im = columns(k)
                out_copy(b, k).wait_recv()
                qg_ref[line, re] = s["o_r"][b, k, :, :wide]
                qg_ref[line, im] = s["o_r"][b, k, :, wide:]
        for b in range(BLOCKS):
            cot_copy(b).wait_send()
            for k in range(CHUNKS):
                g_copy(b, k).wait_send()
                out_copy(b, k).wait_send()
        for drain in drains:
            drain()
        for out in outs:
            out.wait_send()
        x_copy.wait()
        wg_ref[...] = (total[pl.ds(pl.multiple_of(x * 16, 16), 16)] + s["x_r"][...].astype(F32)) * scale
        rel_out(1, 1 - x, 1 - x, 2, other_x).wait_recv()
        finish_rel(s["rel_s"][NX + x] + s["rel_r"][1 - x])


def local(section_rows, weights, relation_table, relation_ids):
    tokens, width = section_rows.shape[1:]
    rels = relation_table.shape[0]
    total = tokens * lax.axis_size("batch")
    half = width // 2
    wide = half // CHUNKS
    block = tokens // BLOCKS
    piece = width // 2 // PIECES
    V = pltpu.VMEM
    D = pltpu.SemaphoreType.DMA
    chunks = (BLOCKS, CHUNKS, block, 2 * wide)

    scratch = {
        "w": V((width, width), BF),
        "table": V((rels, width), BF),
        "w_sem": D((2 * CHUNKS,)),
        "table_sem": D,
        "hop_sem": D((2, BLOCKS, CHUNKS)),
        "out_sem": D((2, BLOCKS, CHUNKS)),
        "cot_sem": D((2, BLOCKS)),
        "ids_sem": D((2,)),
        "right0_sem": D((2, 3)),
        "right1_sem": D((2, BLOCKS)),
        "left0_sem": D((2, CHUNKS, 3)),
        "left1_sem": D((2, CHUNKS)),
        "rel_sem": D((2, 4)),
        "x_sem": D((2,)),
        "q_s": V(chunks, BF),
        "q_r": V(chunks, BF),
        "g_s": V(chunks, BF),
        "g_r": V(chunks, BF),
        "o_r": V(chunks, BF),
        "cot": V((tokens, width), BF),
        "ids": V((1, tokens), jnp.int32),
        "rel": V((tokens, width), BF),
        "mixed": V((tokens, width), BF),
        "pre": V((tokens, width), F32),
        "turned": V((2, NY // 2, NZ, NX, NC, 16, tokens), BF),
        "left0": V((2, NY // 2, NZ, 16, 4 * tokens), BF),
        "right0": V((4 * tokens, width), BF),
        "left1": V((2, NY // 2, NZ, NX, 16, 2 * tokens), BF),
        "right1": V((2 * tokens, width), BF),
        "rp": V((NY, NZ, 8, half), F32),
        "rp_s": V((NY, NZ, 8, half), BF),
        "rp_r": V((NY, NZ, 8, half), BF),
        "rsum_z": V((NY, 8, half // 2), F32),
        "rsum_y": V((NZ, 8, half // 2), F32),
        "rtotal": V((8, half), F32),
        "x_s": V((16, width), BF),
        "x_r": V((16, width), BF),
        "rel_s": V((2 * NX, 2, half), F32),
        "rel_r": V((NX, 2, half), F32),
    }

    def ring_bufs(name, lead, n, rows, cols):
        h = n // 2
        for side in "sr":
            scratch[name + "_" + side + "f"] = V(lead + (2, rows, cols // 2), BF)
            scratch[name + "_" + side + "n"] = V(lead + (2, h - 1, rows, cols), BF)
            scratch[name + "_" + side + "s"] = D(lead + (2, h))

    for name, rows in (("h0", 16), ("h1", NX * 16)):
        ring_bufs(name + "_az", (PIECES,), NZ, NY * rows, piece)
        ring_bufs(name + "_ay", (PIECES,), NY, rows, piece)
        ring_bufs(name + "_by", (PIECES,), NY, NZ * rows, piece)
        ring_bufs(name + "_bz", (PIECES,), NZ, rows, piece)
        scratch[name + "_sum_z"] = V((NY, rows, half), F32)
        scratch[name + "_sum_y"] = V((NZ, rows, half), F32)
        scratch[name + "_total"] = V((rows, width), F32)
    ring_bufs("raz", (), NZ, NY * 8, half // 2)
    ring_bufs("ray", (), NY, 8, half // 2)
    ring_bufs("rby", (), NY, NZ * 8, half // 2)
    ring_bufs("rbz", (), NZ, 8, half // 2)
    names = list(scratch)

    def body(*refs):
        kernel(total, *refs[:7], dict(zip(names, refs[7:])))

    vmem = pl.BlockSpec(memory_space=pltpu.VMEM)
    hbm = pl.BlockSpec(memory_space=pl.ANY)
    wg, rg, qg = pl.pallas_call(
        body,
        out_shape=(
            jax.ShapeDtypeStruct((16, width), F32),
            jax.ShapeDtypeStruct((1, width), F32),
            jax.ShapeDtypeStruct((tokens, width), BF),
        ),
        in_specs=[vmem, hbm, hbm, vmem],
        out_specs=(vmem, vmem, vmem),
        scratch_shapes=[scratch[n] for n in names],
        compiler_params=pltpu.CompilerParams(
            collective_id=0, has_side_effects=True, vmem_limit_bytes=60 * 1024 * 1024
        ),
        name="backward",
    )(section_rows[0], weights[0], relation_table, relation_ids.reshape(1, tokens))
    return (wg[None], rg, qg)


def solution(mesh):
    return jax.shard_map(
        local,
        mesh=mesh,
        in_specs=(P("hop", "batch", None), P("hop", None, None), P(), P("batch")),
        out_specs=(P("hop", "batch", None), P(("hop", "batch"), None), P("batch", None)),
        check_vma=False,
    )
```

```python
import functools
import math

import jax
import jax.numpy as jnp
from jax import lax
from jax.experimental import pallas as pl
from jax.experimental.pallas import tpu as pltpu
from jax.sharding import PartitionSpec as P

MESH = pl.DeviceIdType.MESH
BF = jnp.bfloat16
F32 = jnp.float32
NY, NZ, NX, NC = 4, 8, 2, 2
CHUNKS = 4
PIECES = 2
BLOCKS = 2
Z_FIRST = (0, 4, 10, 16, 22, 22.5, 26, 29, 32)
Y_FIRST = (0, 7, 19, 19.5, 22.2, 25, 28, 30, 33)
RELATION = (1.5, 5.5, 14.5, 14.6, 18.1, 21.1, 24.1, 27.1, 31.1)


def dot(a, b):
    return jnp.dot(a, b, preferred_element_type=F32)


def dot_t(a, b):
    return lax.dot_general(a, b, (((1,), (1,)), ((), ())), preferred_element_type=F32)


def remote(src, dst, send, recv, device):
    return pltpu.make_async_remote_copy(
        src_ref=src, dst_ref=dst, send_sem=send, recv_sem=recv,
        device_id=device, device_id_type=MESH,
    )


def ring(n, index, own, send_far, send_near, recv_far, recv_near, ssem, rsem, devices, finish):
    half = n // 2
    cut = send_far.shape[-1]

    def copy(way, step):
        src = send_far.at[way] if step == 1 else send_near.at[way, step - 2]
        dst = recv_far.at[way] if step == 1 else recv_near.at[way, step - 2]
        return remote(src, dst, ssem.at[way, step - 1], rsem.at[way, step - 1], devices[way])

    def first():
        block = own(lax.rem(index + half, n)).astype(BF)
        send_far[0] = block[:, :cut]
        copy(0, 1).start()
        send_far[1] = block[:, cut:]
        copy(1, 1).start()

    def middle(step):
        distance = half + 1 - step
        for way in (0, 1):
            target = lax.rem(index + (distance if way == 0 else n - distance), n)
            block = own(target)
            copy(way, step - 1).wait_recv()
            if step == 2:
                got = recv_far[way].astype(F32)
                low, high = block[:, :cut], block[:, cut:]
                low, high = (low + got, high) if way == 0 else (low, high + got)
                send_near[way, 0, :, :cut] = low.astype(BF)
                send_near[way, 0, :, cut:] = high.astype(BF)
            else:
                got = recv_near[way, step - 3].astype(F32)
                send_near[way, step - 2] = (block + got).astype(BF)
            copy(way, step).start()

    def last():
        block = own(index)
        copy(0, half).wait_recv()
        copy(1, half).wait_recv()
        finish(block + recv_near[0, half - 2].astype(F32) + recv_near[1, half - 2].astype(F32))

    def drain():
        for step in range(1, half + 1):
            for way in (0, 1):
                copy(way, step).wait_send()

    return [first] + [functools.partial(middle, t) for t in range(2, half + 1)] + [last], drain


def play(streams):
    events = []
    for times, steps in streams:
        events += [(t, len(events) + n, step) for n, (t, step) in enumerate(zip(times, steps))]
    for _, _, step in sorted(events, key=lambda e: e[:2]):
        step()


def kernel(rows_total, rows_ref, w_ref, table_ref, ids_ref, wg_ref, rg_ref, qg_ref, s):
    hop = lax.axis_index("hop")
    place = lax.axis_index("batch")
    core = lax.rem(place, NC)
    x = lax.rem(place // NC, NX)
    z = lax.rem(place // (NC * NX), NZ)
    y = place // (NC * NX * NZ)

    def at(h, yy, zz, xx, cc):
        return (h, ((yy * NZ + zz) * NX + xx) * NC + cc)

    other_core = at(hop, y, z, x, 1 - core)
    other_hop = at(1 - hop, y, z, x, core)
    other_x = at(hop, y, z, 1 - x, core)
    diagonal = at(hop, y, z, 1 - x, 1 - core)
    across = at(1 - hop, y, z, 1 - x, core)
    y_ways = (at(hop, lax.rem(y + 1, NY), z, x, core), at(hop, lax.rem(y + NY - 1, NY), z, x, core))
    z_ways = (at(hop, y, lax.rem(z + 1, NZ), x, core), at(hop, y, lax.rem(z + NZ - 1, NZ), x, core))

    tokens, width = rows_ref.shape
    block = tokens // BLOCKS
    half = width // 2
    wide = half // CHUNKS
    rels = table_ref.shape[0]
    colour = width // 2
    piece = colour // PIECES
    group = NZ * (NY // 2) // CHUNKS

    def w_copy(j):
        part = pl.ds(j * wide, wide)
        return pltpu.make_async_copy(w_ref.at[part], s["w"].at[part], s["w_sem"].at[j])

    table_copy = pltpu.make_async_copy(table_ref, s["table"], s["table_sem"])
    for k in range(CHUNKS):
        w_copy(k).start()
        w_copy(k + CHUNKS).start()
    table_copy.start()

    y_far = at(hop, lax.rem(y + NY // 2, NY), z, x, core)
    partners = (other_core, other_hop, other_x, diagonal, across, y_far) + y_ways + z_ways
    barrier = pltpu.get_barrier_semaphore()
    for device in partners:
        pl.semaphore_signal(barrier, inc=1, device_id=device, device_id_type=MESH)
    pl.semaphore_wait(barrier, len(partners))

    w, turned = s["w"], s["turned"]

    def hop_copy(src, dst, b, k):
        return remote(s[src].at[b, k], s[dst].at[b, k], s["hop_sem"].at[0, b, k], s["hop_sem"].at[1, b, k], across)

    def q_copy(b, k):
        return hop_copy("q_s", "q_r", b, k)

    def g_copy(b, k):
        return hop_copy("g_s", "g_r", b, k)

    def spot(k):
        return k // (CHUNKS // 2), k % (CHUNKS // 2) * group

    def turn(k, re, im):
        low, z0 = spot(k)
        for part, values in enumerate((re, im)):
            flat = values.astype(F32).T.astype(BF)
            for g in range(group):
                for xx in range(NX):
                    for cc in range(NC):
                        row = ((g * NX + xx) * NC + cc) * 16
                        turned[part, low, z0 + g, xx, cc] = flat[row:row + 16]

    def bufs(name):
        return [s[name + "_" + b] for b in ("sf", "sn", "rf", "rn", "ss", "rs")]

    def sub(refs, p):
        return [r.at[p] for r in refs]

    def weight_rings(name, left, right, rows, streams, drains, end):
        depth = right.shape[0]

        def by_z(cols):
            def own(zz):
                a = left[:, :, zz].reshape(NY * rows, depth)
                return dot(a, right[:, cols])
            return own

        def by_y(cols):
            def own(yy):
                a = left[yy // 2, lax.rem(yy, 2)].reshape(NZ * rows, depth)
                return dot(a, right[:, cols])
            return own

        for p in range(PIECES):
            here = slice(p * piece, (p + 1) * piece)
            cols = (here, slice(colour + p * piece, colour + (p + 1) * piece))

            def keep_z(v, here=here):
                s[name + "_sum_z"][:, :, here] = v.reshape(NY, rows, piece)

            def keep_y(v, here=here):
                s[name + "_sum_y"][:, :, here] = v.reshape(NZ, rows, piece)

            def from_z(yy, here=here):
                return s[name + "_sum_z"][yy, :, here]

            def from_y(zz, here=here):
                return s[name + "_sum_y"][zz, :, here]

            last_z, more_z = end(p, 0, cols[0])
            last_y, more_y = end(p, 1, cols[1])
            one = ring(NZ, z, by_z(cols[0]), *sub(bufs(name + "_az"), p), z_ways, keep_z)
            two = ring(NY, y, from_z, *sub(bufs(name + "_ay"), p), y_ways, last_z)
            three = ring(NY, y, by_y(cols[1]), *sub(bufs(name + "_by"), p), y_ways, keep_y)
            four = ring(NZ, z, from_y, *sub(bufs(name + "_bz"), p), z_ways, last_y)
            streams.append(([t + 0.5 * p for t in Z_FIRST], one[0] + two[0] + more_z))
            streams.append(([t + 0.5 * p + 0.25 for t in Y_FIRST], three[0] + four[0] + more_y))
            drains += [one[1], two[1], three[1], four[1]]

    scale = 1.0 / math.sqrt(rows_total)
    rel_scale = math.sqrt(rels / rows_total)

    def rel_copy(src, slot, sem, device):
        return remote(s["rel_s"].at[src], s["rel_r"].at[slot], s["rel_sem"].at[0, sem], s["rel_sem"].at[1, sem], device)

    def rel_y_copy(n):
        target = lax.rem(y + n, NY)
        return remote(
            s["rel_o"].at[target], s["rel_i"].at[n - 1], s["rel_y_sem"].at[0, n - 1], s["rel_y_sem"].at[1, n - 1],
            (y_ways[0], y_far, y_ways[1])[n - 1],
        )

    def rel_tail(drains):
        def own(zz):
            return s["rp"][zz]

        def split(v):
            for yy in range(NY):
                for side in range(2):
                    s["rel_o"][yy, side:side + 1] = v[yy * 2 + side:yy * 2 + side + 1]
            for n in range(1, NY):
                rel_y_copy(n).start()

        def final():
            for n in range(1, NY):
                rel_y_copy(n).wait_recv()
            total = s["rel_o"][y] + s["rel_i"][0] + s["rel_i"][1] + s["rel_i"][2]
            rg_ref[:, :half] = total[0:1] * rel_scale
            rg_ref[:, half:] = total[1:2] * rel_scale

        steps, drain = ring(NZ, z, own, *bufs("rz"), z_ways, split)
        drains.append(drain)
        drains.append(lambda: [rel_y_copy(n).wait_send() for n in range(1, NY)])
        return steps + [final]

    @pl.when(hop == 0)
    def _():
        left, right = s["left0"], s["right0"]
        dest = (None, other_core, other_x, diagonal)

        def slot(n):
            return right.at[pl.ds(n * tokens, tokens)]

        sends = s["right0_sem"]
        to_core = remote(rows_ref, slot(1), sends.at[0, 0], sends.at[1, 0], other_core)
        to_x = remote(rows_ref, slot(2), sends.at[0, 1], sends.at[1, 1], other_x)
        onward = remote(slot(2), slot(3), sends.at[0, 2], sends.at[1, 2], other_core)
        to_x.start()

        for k in range(CHUNKS):
            for part in range(2):
                w_copy(k + part * CHUNKS).wait()
                weight = w[pl.ds(part * half + k * wide, wide)]
                q = dot_t(rows_ref[...], weight).astype(BF)
                for b in range(BLOCKS):
                    s["q_s"][b, k, :, part * wide:(part + 1) * wide] = q[b * block:(b + 1) * block]
            q_copy(0, k).start()
        for b in range(1, BLOCKS):
            for k in range(CHUNKS):
                q_copy(b, k).start()
        to_core.start()
        right[0:tokens] = rows_ref[...]
        table_copy.wait()

        def left_copy(k, n):
            low, z0 = spot(k)
            xx, cc = (x, 1 - core) if n == 1 else (1 - x, core if n == 2 else 1 - core)
            return remote(
                turned.at[:, low, pl.ds(z0, group), xx, cc],
                left.at[:, low, pl.ds(z0, group), :, pl.ds(n * tokens, tokens)],
                s["left0_sem"].at[0, k, n - 1], s["left0_sem"].at[1, k, n - 1], dest[n],
            )

        for b in range(BLOCKS):
            line = slice(b * block, (b + 1) * block)
            for k in range(CHUNKS):
                re = slice(k * wide, (k + 1) * wide)
                im = slice(half + k * wide, half + (k + 1) * wide)
                g_copy(b, k).wait_recv()
                qg_ref[line, re] = s["g_r"][b, k, :, :wide]
                qg_ref[line, im] = s["g_r"][b, k, :, wide:]
                if b == BLOCKS - 1:
                    low, z0 = spot(k)
                    turn(k, qg_ref[:, re], qg_ref[:, im])
                    for n in (2, 3, 1):
                        left_copy(k, n).start()
                    left[:, low, z0:z0 + group, :, 0:tokens] = turned[:, low, z0:z0 + group, x, core]
            if b == 0:
                to_x.wait_recv()
                onward.start()
        to_core.wait()
        to_x.wait_send()
        onward.wait()
        for k in range(CHUNKS):
            for n in (1, 2, 3):
                left_copy(k, n).wait()

        streams, drains = [], []

        def end(p, which, cols):
            def last(v):
                wg_ref[:, cols] = v * scale
            return last, []

        def rel_take():
            for slot in range(NX):
                rel_copy(0, slot, slot, across).wait_recv()
            s["rp"][...] = s["rel_r"][0].astype(F32) + s["rel_r"][1].astype(F32)

        weight_rings("h0", left, right, 16, streams, drains, end)
        streams.append((RELATION[2:], [rel_take] + rel_tail(drains)))
        play(streams)
        for b in range(BLOCKS):
            for k in range(CHUNKS):
                q_copy(b, k).wait_send()
        for drain in drains:
            drain()

    @pl.when(hop == 1)
    def _():
        left, right = s["left1"], s["right1"]

        def cot_copy(b):
            line = pl.ds(b * block, block)
            return remote(rows_ref.at[line], s["cot"].at[line], s["cot_sem"].at[0, b], s["cot_sem"].at[1, b], other_x)

        def out_copy(b, k):
            return remote(s["g_s"].at[b, k], s["o_r"].at[b, k], s["out_sem"].at[0, b, k], s["out_sem"].at[1, b, k], other_x)

        def right_copy(b):
            return remote(
                right.at[pl.ds(b * block, block)], right.at[pl.ds(tokens + b * block, block)],
                s["right1_sem"].at[0, b], s["right1_sem"].at[1, b], other_core,
            )

        def left_copy(k):
            low, z0 = spot(k)
            return remote(
                turned.at[:, low, pl.ds(z0, group), :, 1 - core],
                left.at[:, low, pl.ds(z0, group), :, :, pl.ds(tokens, tokens)],
                s["left1_sem"].at[0, k], s["left1_sem"].at[1, k], other_core,
            )

        ids_copy = remote(ids_ref, s["ids"], s["ids_sem"].at[0], s["ids_sem"].at[1], other_x)
        ids_copy.start()
        for b in range(BLOCKS):
            cot_copy(b).start()
        ids_copy.wait()
        ids = s["ids"][...]
        rows_of = lax.broadcasted_iota(jnp.int32, (rels, tokens), 0)
        onehot = jnp.where(rows_of == ids, 1.0, 0.0).T.astype(BF)
        table_copy.wait()
        for n in range(CHUNKS):
            part = slice(n * 2 * wide, (n + 1) * 2 * wide)
            s["rel"][:, part] = dot(onehot, s["table"][:, part]).astype(BF)
        for k in range(CHUNKS):
            w_copy(k).wait()
            w_copy(k + CHUNKS).wait()

        def columns(k):
            return slice(k * wide, (k + 1) * wide), slice(half + k * wide, half + (k + 1) * wide)

        def forward(b, k):
            re, im = columns(k)
            line = slice(b * block, (b + 1) * block)
            r_re, r_im = s["rel"][line, re].astype(F32), s["rel"][line, im].astype(F32)
            q_copy(b, k).wait_recv()
            q_re = s["q_r"][b, k, :, :wide].astype(F32)
            q_im = s["q_r"][b, k, :, wide:].astype(F32)
            z_re = (q_re * r_re - q_im * r_im).astype(BF)
            z_im = (q_re * r_im + q_im * r_re).astype(BF)
            s["mixed"][line, re] = z_re
            s["mixed"][line, im] = z_im
            for n in range(CHUNKS):
                part = slice(n * 2 * wide, (n + 1) * 2 * wide)
                term = dot(z_re, w[re, part]) + dot(z_im, w[im, part])
                s["pre"][line, part] = term if k == 0 else s["pre"][line, part] + term

        def activate(b):
            line = slice(b * block, (b + 1) * block)
            cot_copy(b).wait_recv()
            for n in range(CHUNKS):
                part = slice(n * 2 * wide, (n + 1) * 2 * wide)
                pre = s["pre"][line, part]
                sig = 1.0 / (1.0 + jnp.exp(-pre))
                slope = sig * (1.0 + pre * (1.0 - sig))
                right[line, part] = (s["cot"][line, part].astype(F32) * slope).astype(BF)
            right_copy(b).start()

        def back(b, k):
            re, im = columns(k)
            line = slice(b * block, (b + 1) * block)
            g_a = right[line]
            gz_re = dot_t(g_a, w[re])
            gz_im = dot_t(g_a, w[im])
            r_re, r_im = s["rel"][line, re].astype(F32), s["rel"][line, im].astype(F32)
            s["g_s"][b, k, :, :wide] = (gz_re * r_re + gz_im * r_im).astype(BF)
            s["g_s"][b, k, :, wide:] = (gz_im * r_re - gz_re * r_im).astype(BF)
            g_copy(b, k).start()
            q_re = s["q_r"][b, k, :, :wide].astype(F32)
            q_im = s["q_r"][b, k, :, wide:].astype(F32)
            s["pre"][line, re] = gz_re * q_re + gz_im * q_im
            s["pre"][line, im] = gz_im * q_re - gz_re * q_im

        def share(k):
            re, im = columns(k)
            low, z0 = spot(k)
            turn(k, s["mixed"][:, re], s["mixed"][:, im])
            left_copy(k).start()
            left[:, low, z0:z0 + group, :, :, 0:tokens] = turned[:, low, z0:z0 + group, :, core]

        for b in range(BLOCKS):
            for k in range(CHUNKS):
                forward(b, k)
                if b == BLOCKS - 1:
                    share(k)
            activate(b)
            for k in range(CHUNKS):
                back(b, k)
        for b in range(BLOCKS):
            right_copy(b).wait()
        for k in range(CHUNKS):
            left_copy(k).wait()

        swap = remote(s["rp_s"], s["rp_r"], s["rel_sem"].at[0, 3], s["rel_sem"].at[1, 3], other_core)
        aims = ((0, x, other_hop), (1, 1 - x, across), (2, 1 - x, other_x))

        def rel_start():
            row = lax.broadcasted_iota(jnp.int32, (rels, tokens), 0)
            side_of = lax.rem(row, 2)
            yy, zz = lax.rem(row // 2, NY), lax.rem(row // (2 * NY), NZ)
            hx = row // (2 * NY * NZ)
            base = (hx // NX) * (rels // 2) + ((yy * NZ + zz) * NX + lax.rem(hx, NX)) * NC
            who = s["ids"][...]

            def partial_for(which):
                match = jnp.where(base + which == who, 1.0, 0.0)
                total = None
                for side in range(2):
                    pick = jnp.where(side_of == side, match, 0.0).astype(BF)
                    values = s["pre"][:, side * half:(side + 1) * half]
                    head = values.astype(BF)
                    tail = (values - head.astype(F32)).astype(BF)
                    term = dot(pick, head) + dot(pick, tail)
                    total = term if total is None else total + term
                return total.reshape(2 * NX, NZ, 2 * NY, half)

            s["rp_s"][...] = partial_for(1 - core).astype(BF)
            swap.start()
            s["rp_o"][...] = partial_for(core)

        def rel_send(n):
            if n == 0:
                return remote(s["rel_s"].at[x], s["rel_r"].at[x], s["rel_sem"].at[0, 0], s["rel_sem"].at[1, x], other_hop)
            if n == 1:
                return remote(s["rel_s"].at[1 - x], s["rel_r"].at[x], s["rel_sem"].at[0, 1], s["rel_sem"].at[1, x], across)
            return remote(s["rel_s"].at[NX + 1 - x], s["rel_r"].at[0], s["rel_sem"].at[0, 2], s["rel_sem"].at[1, 2], other_x)

        def rel_join():
            swap.wait()
            for n in range(2 * NX):
                s["rel_s"][n] = (s["rp_o"][n] + s["rp_r"][n].astype(F32)).astype(BF)
            s["rp"][...] = s["rp_o"][NX + x] + s["rp_r"][NX + x].astype(F32)
            for n in range(3):
                rel_send(n).start()
            for b in range(BLOCKS):
                for k in range(CHUNKS):
                    out_copy(b, k).start()

        def rel_take():
            rel_send(2).wait_recv()
            s["rp"][...] = s["rp"][...] + s["rel_r"][0].astype(F32)

        def x_copy(p, which):
            return remote(
                s["x_s"].at[which, p], s["x_r"].at[which, p],
                s["x_sem"].at[0, which, p], s["x_sem"].at[1, which, p], other_x,
            )

        def end(p, which, cols):
            def last(v):
                s["total"][which, p] = v.reshape(NX, 16, piece)
                s["x_s"][which, p] = s["total"][which, p, 1 - x].astype(BF)
                x_copy(p, which).start()

            def more():
                x_copy(p, which).wait_recv()
                wg_ref[:, cols] = (s["total"][which, p, x] + s["x_r"][which, p].astype(F32)) * scale

            return last, [more]

        streams, drains = [], []
        weight_rings("h1", left, right, NX * 16, streams, drains, end)
        streams.append((RELATION, [rel_start, rel_join, rel_take] + rel_tail(drains)))
        play(streams)

        for b in range(BLOCKS):
            line = slice(b * block, (b + 1) * block)
            for k in range(CHUNKS):
                re, im = columns(k)
                out_copy(b, k).wait_recv()
                qg_ref[line, re] = s["o_r"][b, k, :, :wide]
                qg_ref[line, im] = s["o_r"][b, k, :, wide:]
        for b in range(BLOCKS):
            cot_copy(b).wait_send()
            for k in range(CHUNKS):
                g_copy(b, k).wait_send()
                out_copy(b, k).wait_send()
        for drain in drains:
            drain()
        for n in range(3):
            rel_send(n).wait_send()
        for which in range(2):
            for p in range(PIECES):
                x_copy(p, which).wait_send()


def settle(wg_in, rg_in, qg_in, wg_out, rg_out, qg_out):
    wg_out[0] = wg_in[...]
    rg_out[...] = rg_in[...]
    qg_out[...] = qg_in[...]


def local(section_rows, weights, relation_table, relation_ids):
    tokens, width = section_rows.shape[1:]
    rels = relation_table.shape[0]
    total = tokens * lax.axis_size("batch")
    half = width // 2
    wide = half // CHUNKS
    block = tokens // BLOCKS
    piece = width // 2 // PIECES
    V = pltpu.VMEM
    D = pltpu.SemaphoreType.DMA
    chunks = (BLOCKS, CHUNKS, block, 2 * wide)

    scratch = {
        "w": V((width, width), BF),
        "table": V((rels, width), BF),
        "w_sem": D((2 * CHUNKS,)),
        "table_sem": D,
        "hop_sem": D((2, BLOCKS, CHUNKS)),
        "out_sem": D((2, BLOCKS, CHUNKS)),
        "cot_sem": D((2, BLOCKS)),
        "ids_sem": D((2,)),
        "right0_sem": D((2, 3)),
        "right1_sem": D((2, BLOCKS)),
        "left0_sem": D((2, CHUNKS, 3)),
        "left1_sem": D((2, CHUNKS)),
        "rel_sem": D((2, 4)),
        "x_sem": D((2, 2, PIECES)),
        "q_s": V(chunks, BF),
        "q_r": V(chunks, BF),
        "g_s": V(chunks, BF),
        "g_r": V(chunks, BF),
        "o_r": V(chunks, BF),
        "cot": V((tokens, width), BF),
        "ids": V((1, tokens), jnp.int32),
        "rel": V((tokens, width), BF),
        "mixed": V((tokens, width), BF),
        "pre": V((tokens, width), F32),
        "turned": V((2, NY // 2, NZ, NX, NC, 16, tokens), BF),
        "left0": V((2, NY // 2, NZ, 16, 4 * tokens), BF),
        "right0": V((4 * tokens, width), BF),
        "left1": V((2, NY // 2, NZ, NX, 16, 2 * tokens), BF),
        "right1": V((2 * tokens, width), BF),
        "rp": V((NZ, 2 * NY, half), F32),
        "rp_o": V((2 * NX, NZ, 2 * NY, half), F32),
        "rp_s": V((2 * NX, NZ, 2 * NY, half), BF),
        "rp_r": V((2 * NX, NZ, 2 * NY, half), BF),
        "rel_s": V((2 * NX, NZ, 2 * NY, half), BF),
        "rel_r": V((NX, NZ, 2 * NY, half), BF),
        "rel_o": V((NY, 2, half), F32),
        "rel_i": V((NY - 1, 2, half), F32),
        "rel_y_sem": D((2, NY - 1)),
        "total": V((2, PIECES, NX, 16, piece), F32),
        "x_s": V((2, PIECES, 16, piece), BF),
        "x_r": V((2, PIECES, 16, piece), BF),
    }

    def ring_bufs(name, lead, n, rows, cols):
        h = n // 2
        for side in "sr":
            scratch[name + "_" + side + "f"] = V(lead + (2, rows, cols // 2), BF)
            scratch[name + "_" + side + "n"] = V(lead + (2, h - 1, rows, cols), BF)
            scratch[name + "_" + side + "s"] = D(lead + (2, h))

    for name, rows in (("h0", 16), ("h1", NX * 16)):
        ring_bufs(name + "_az", (PIECES,), NZ, NY * rows, piece)
        ring_bufs(name + "_ay", (PIECES,), NY, rows, piece)
        ring_bufs(name + "_by", (PIECES,), NY, NZ * rows, piece)
        ring_bufs(name + "_bz", (PIECES,), NZ, rows, piece)
        scratch[name + "_sum_z"] = V((NY, rows, half), F32)
        scratch[name + "_sum_y"] = V((NZ, rows, half), F32)
    ring_bufs("rz", (), NZ, 2 * NY, half)
    names = list(scratch)

    def body(*refs):
        kernel(total, *refs[:7], dict(zip(names, refs[7:])))

    vmem = pl.BlockSpec(memory_space=pltpu.VMEM)
    hbm = pl.BlockSpec(memory_space=pl.ANY)
    wg, rg, qg = pl.pallas_call(
        body,
        out_shape=(
            jax.ShapeDtypeStruct((16, width), F32),
            jax.ShapeDtypeStruct((1, width), F32),
            jax.ShapeDtypeStruct((tokens, width), BF),
        ),
        in_specs=[vmem, hbm, hbm, vmem],
        out_specs=(vmem, vmem, vmem),
        scratch_shapes=[scratch[n] for n in names],
        compiler_params=pltpu.CompilerParams(
            collective_id=0, has_side_effects=True, vmem_limit_bytes=60 * 1024 * 1024
        ),
        name="backward",
    )(section_rows[0], weights[0], relation_table, relation_ids.reshape(1, tokens))
    shapes = (
        jax.ShapeDtypeStruct((1, 16, width), F32),
        jax.ShapeDtypeStruct((1, width), F32),
        jax.ShapeDtypeStruct((tokens, width), BF),
    )
    return pl.pallas_call(
        settle, out_shape=shapes, in_specs=[vmem] * 3, out_specs=(vmem, vmem, vmem), name="settle"
    )(wg, rg, qg)


def solution(mesh):
    return jax.shard_map(
        local,
        mesh=mesh,
        in_specs=(P("hop", "batch", None), P("hop", None, None), P(), P("batch")),
        out_specs=(P("hop", "batch", None), P(("hop", "batch"), None), P("batch", None)),
        check_vma=False,
    )
```

```python
import functools
import math

import jax
import jax.numpy as jnp
from jax import lax
from jax.experimental import pallas as pl
from jax.experimental.pallas import tpu as pltpu
from jax.sharding import PartitionSpec as P

MESH = pl.DeviceIdType.MESH
BF = jnp.bfloat16
F32 = jnp.float32
NY, NZ, NX, NC = 4, 8, 2, 2
CHUNKS = 4
PIECES = 2
SIZES = (64, 64)
BLOCKS = len(SIZES)
STARTS = tuple(sum(SIZES[:n]) for n in range(BLOCKS))
Z_FIRST = (0, 4, 10, 16, 22, 22.5, 26, 29, 32)
Y_FIRST = (0, 7, 19, 19.5, 22.2, 25, 28, 30, 33)
RELATION = (1.5, 5.5, 14.5, 14.6, 18.1, 21.1, 24.1, 27.1, 31.1)


def dot(a, b):
    return jnp.dot(a, b, preferred_element_type=F32)


def dot_t(a, b):
    return lax.dot_general(a, b, (((1,), (1,)), ((), ())), preferred_element_type=F32)


def remote(src, dst, send, recv, device):
    return pltpu.make_async_remote_copy(
        src_ref=src, dst_ref=dst, send_sem=send, recv_sem=recv,
        device_id=device, device_id_type=MESH,
    )


def ring(n, index, own, send_far, send_near, recv_far, recv_near, ssem, rsem, devices, finish):
    half = n // 2
    cut = send_far.shape[-1]

    def copy(way, step):
        src = send_far.at[way] if step == 1 else send_near.at[way, step - 2]
        dst = recv_far.at[way] if step == 1 else recv_near.at[way, step - 2]
        return remote(src, dst, ssem.at[way, step - 1], rsem.at[way, step - 1], devices[way])

    def first():
        block = own(lax.rem(index + half, n)).astype(BF)
        send_far[0] = block[:, :cut]
        copy(0, 1).start()
        send_far[1] = block[:, cut:]
        copy(1, 1).start()

    def middle(step):
        distance = half + 1 - step
        for way in (0, 1):
            target = lax.rem(index + (distance if way == 0 else n - distance), n)
            block = own(target)
            copy(way, step - 1).wait_recv()
            if step == 2:
                got = recv_far[way].astype(F32)
                low, high = block[:, :cut], block[:, cut:]
                low, high = (low + got, high) if way == 0 else (low, high + got)
                send_near[way, 0, :, :cut] = low.astype(BF)
                send_near[way, 0, :, cut:] = high.astype(BF)
            else:
                got = recv_near[way, step - 3].astype(F32)
                send_near[way, step - 2] = (block + got).astype(BF)
            copy(way, step).start()

    def last():
        block = own(index)
        copy(0, half).wait_recv()
        copy(1, half).wait_recv()
        finish(block + recv_near[0, half - 2].astype(F32) + recv_near[1, half - 2].astype(F32))

    def drain():
        for step in range(1, half + 1):
            for way in (0, 1):
                copy(way, step).wait_send()

    return [first] + [functools.partial(middle, t) for t in range(2, half + 1)] + [last], drain


def play(streams):
    events = []
    for times, steps in streams:
        events += [(t, len(events) + n, step) for n, (t, step) in enumerate(zip(times, steps))]
    for _, _, step in sorted(events, key=lambda e: e[:2]):
        step()


def kernel(rows_total, rows_hbm, w_ref, table_ref, ids_ref, wg_hbm, rg_hbm, qg_hbm, s):
    hop = lax.axis_index("hop")
    place = lax.axis_index("batch")
    core = lax.rem(place, NC)
    x = lax.rem(place // NC, NX)
    z = lax.rem(place // (NC * NX), NZ)
    y = place // (NC * NX * NZ)

    def at(h, yy, zz, xx, cc):
        return (h, ((yy * NZ + zz) * NX + xx) * NC + cc)

    other_core = at(hop, y, z, x, 1 - core)
    other_hop = at(1 - hop, y, z, x, core)
    other_x = at(hop, y, z, 1 - x, core)
    diagonal = at(hop, y, z, 1 - x, 1 - core)
    across = at(1 - hop, y, z, 1 - x, core)
    y_ways = (at(hop, lax.rem(y + 1, NY), z, x, core), at(hop, lax.rem(y + NY - 1, NY), z, x, core))
    z_ways = (at(hop, y, lax.rem(z + 1, NZ), x, core), at(hop, y, lax.rem(z + NZ - 1, NZ), x, core))

    rows_ref, wg_ref, rg_ref = s["rows"], s["wg"], s["rg"]
    tokens, width = rows_ref.shape
    half = width // 2
    wide = half // CHUNKS
    rels = table_ref.shape[0]
    colour = width // 2
    piece = colour // PIECES
    group = NZ * (NY // 2) // CHUNKS

    def w_copy(j):
        part = pl.ds(j * wide, wide)
        return pltpu.make_async_copy(w_ref.at[part], s["w"].at[part], s["w_sem"].at[j])

    table_copy = pltpu.make_async_copy(table_ref, s["table"], s["table_sem"])
    rows_copy = pltpu.make_async_copy(rows_hbm, rows_ref, s["rows_sem"])
    rows_copy.start()
    w_copy(0).start()
    w_copy(CHUNKS).start()

    y_far = at(hop, lax.rem(y + NY // 2, NY), z, x, core)
    partners = (other_core, other_hop, other_x, diagonal, across, y_far) + y_ways + z_ways
    barrier = pltpu.get_barrier_semaphore()
    for device in partners:
        pl.semaphore_signal(barrier, inc=1, device_id=device, device_id_type=MESH)

    def lead(k):
        for part in range(2):
            w_copy(k + part * CHUNKS).wait()
            weight = s["w"][pl.ds(part * half + k * wide, wide)]
            s["q_s"][k, :, part * wide:(part + 1) * wide] = dot_t(rows_ref[...], weight).astype(BF)

    for k in range(1, CHUNKS):
        w_copy(k).start()
        w_copy(k + CHUNKS).start()
    table_copy.start()
    rows_copy.wait()
    pl.when(hop == 0)(lambda: lead(0))
    pl.semaphore_wait(barrier, len(partners))

    w, turned = s["w"], s["turned"]

    def hop_copy(src, dst, b, k):
        line = pl.ds(STARTS[b], SIZES[b])
        return remote(
            s[src].at[k, line], s[dst].at[k, line], s["hop_sem"].at[0, b, k], s["hop_sem"].at[1, b, k], across
        )

    def line_of(b):
        return slice(STARTS[b], STARTS[b] + SIZES[b])

    def out_parts(src, k):
        return [
            pltpu.make_async_copy(
                s[src].at[k, :, pl.ds(part * wide, wide)],
                qg_hbm.at[:, pl.ds(part * half + k * wide, wide)],
                s["qg_sem"].at[k, part],
            )
            for part in range(2)
        ]

    def write_grads():
        pairs = ((wg_ref, wg_hbm, 0), (rg_ref, rg_hbm, 1))
        copies = [pltpu.make_async_copy(src, dst, s["grad_sem"].at[n]) for src, dst, n in pairs]
        for copy in copies:
            copy.start()
        for copy in copies:
            copy.wait()

    def q_copy(b, k):
        return hop_copy("q_s", "q_r", b, k)

    def g_copy(b, k):
        return hop_copy("g_s", "g_r", b, k)

    def spot(k):
        return k // (CHUNKS // 2), k % (CHUNKS // 2) * group

    def turn(k, re, im):
        low, z0 = spot(k)
        for part, values in enumerate((re, im)):
            flat = values.astype(F32).T.astype(BF)
            for g in range(group):
                for xx in range(NX):
                    for cc in range(NC):
                        row = ((g * NX + xx) * NC + cc) * 16
                        turned[part, low, z0 + g, xx, cc] = flat[row:row + 16]

    def bufs(name):
        return [s[name + "_" + b] for b in ("sf", "sn", "rf", "rn", "ss", "rs")]

    def sub(refs, p):
        return [r.at[p] for r in refs]

    def weight_rings(name, left, right, rows, streams, drains, end):
        depth = right.shape[0]

        def by_z(cols):
            def own(zz):
                a = left[:, :, zz].reshape(NY * rows, depth)
                return dot(a, right[:, cols])
            return own

        def by_y(cols):
            def own(yy):
                a = left[yy // 2, lax.rem(yy, 2)].reshape(NZ * rows, depth)
                return dot(a, right[:, cols])
            return own

        for p in range(PIECES):
            here = slice(p * piece, (p + 1) * piece)
            cols = (here, slice(colour + p * piece, colour + (p + 1) * piece))

            def keep_z(v, here=here):
                s[name + "_sum_z"][:, :, here] = v.reshape(NY, rows, piece)

            def keep_y(v, here=here):
                s[name + "_sum_y"][:, :, here] = v.reshape(NZ, rows, piece)

            def from_z(yy, here=here):
                return s[name + "_sum_z"][yy, :, here]

            def from_y(zz, here=here):
                return s[name + "_sum_y"][zz, :, here]

            last_z, more_z = end(p, 0, cols[0])
            last_y, more_y = end(p, 1, cols[1])
            one = ring(NZ, z, by_z(cols[0]), *sub(bufs(name + "_az"), p), z_ways, keep_z)
            two = ring(NY, y, from_z, *sub(bufs(name + "_ay"), p), y_ways, last_z)
            three = ring(NY, y, by_y(cols[1]), *sub(bufs(name + "_by"), p), y_ways, keep_y)
            four = ring(NZ, z, from_y, *sub(bufs(name + "_bz"), p), z_ways, last_y)
            streams.append(([t + 0.5 * p for t in Z_FIRST], one[0] + two[0] + more_z))
            streams.append(([t + 0.5 * p + 0.25 for t in Y_FIRST], three[0] + four[0] + more_y))
            drains += [one[1], two[1], three[1], four[1]]

    scale = 1.0 / math.sqrt(rows_total)
    rel_scale = math.sqrt(rels / rows_total)

    def rel_copy(src, slot, sem, device):
        return remote(s["rel_s"].at[src], s["rel_r"].at[slot], s["rel_sem"].at[0, sem], s["rel_sem"].at[1, sem], device)

    def rel_y_copy(n):
        target = lax.rem(y + n, NY)
        return remote(
            s["rel_o"].at[target], s["rel_i"].at[n - 1], s["rel_y_sem"].at[0, n - 1], s["rel_y_sem"].at[1, n - 1],
            (y_ways[0], y_far, y_ways[1])[n - 1],
        )

    def rel_tail(drains):
        def own(zz):
            return s["rp"][zz]

        def split(v):
            for yy in range(NY):
                for side in range(2):
                    s["rel_o"][yy, side:side + 1] = v[yy * 2 + side:yy * 2 + side + 1]
            for n in range(1, NY):
                rel_y_copy(n).start()

        def final():
            for n in range(1, NY):
                rel_y_copy(n).wait_recv()
            total = s["rel_o"][y] + s["rel_i"][0] + s["rel_i"][1] + s["rel_i"][2]
            rg_ref[:, :half] = total[0:1] * rel_scale
            rg_ref[:, half:] = total[1:2] * rel_scale

        steps, drain = ring(NZ, z, own, *bufs("rz"), z_ways, split)
        drains.append(drain)
        drains.append(lambda: [rel_y_copy(n).wait_send() for n in range(1, NY)])
        return steps + [final]

    @pl.when(hop == 0)
    def _():
        left, right = s["left0"], s["right0"]
        dest = (None, other_core, other_x, diagonal)

        def slot(n):
            return right.at[pl.ds(n * tokens, tokens)]

        sends = s["right0_sem"]
        to_core = remote(rows_ref, slot(1), sends.at[0, 0], sends.at[1, 0], other_core)
        to_x = remote(rows_ref, slot(2), sends.at[0, 1], sends.at[1, 1], other_x)
        onward = remote(slot(2), slot(3), sends.at[0, 2], sends.at[1, 2], other_core)
        to_x.start()

        for k in range(CHUNKS):
            if k:
                lead(k)
            q_copy(0, k).start()
        for b in range(1, BLOCKS):
            for k in range(CHUNKS):
                q_copy(b, k).start()
        to_core.start()
        right[0:tokens] = rows_ref[...]
        table_copy.wait()

        def left_copy(k, n):
            low, z0 = spot(k)
            xx, cc = (x, 1 - core) if n == 1 else (1 - x, core if n == 2 else 1 - core)
            return remote(
                turned.at[:, low, pl.ds(z0, group), xx, cc],
                left.at[:, low, pl.ds(z0, group), :, pl.ds(n * tokens, tokens)],
                s["left0_sem"].at[0, k, n - 1], s["left0_sem"].at[1, k, n - 1], dest[n],
            )

        for b in range(BLOCKS):
            for k in range(CHUNKS):
                g_copy(b, k).wait_recv()
                if b == BLOCKS - 1:
                    low, z0 = spot(k)
                    turn(k, s["g_r"][k, :, :wide], s["g_r"][k, :, wide:])
                    for n in (2, 3, 1):
                        left_copy(k, n).start()
                    left[:, low, z0:z0 + group, :, 0:tokens] = turned[:, low, z0:z0 + group, x, core]
                    for copy in out_parts("g_r", k):
                        copy.start()
            if b == 0:
                to_x.wait_recv()
                onward.start()
        to_core.wait()
        to_x.wait_send()
        onward.wait()
        for k in range(CHUNKS):
            for n in (1, 2, 3):
                left_copy(k, n).wait()

        streams, drains = [], []

        def end(p, which, cols):
            def last(v):
                wg_ref[:, cols] = v * scale
            return last, []

        def rel_take():
            for slot in range(NX):
                rel_copy(0, slot, slot, across).wait_recv()
            s["rp"][...] = s["rel_r"][0].astype(F32) + s["rel_r"][1].astype(F32)

        weight_rings("h0", left, right, 16, streams, drains, end)
        streams.append((RELATION[2:], [rel_take] + rel_tail(drains)))
        play(streams)
        write_grads()
        for k in range(CHUNKS):
            for b in range(BLOCKS):
                q_copy(b, k).wait_send()
            for copy in out_parts("g_r", k):
                copy.wait()
        for drain in drains:
            drain()

    @pl.when(hop == 1)
    def _():
        left, right = s["left1"], s["right1"]

        def cot_copy(b):
            line = pl.ds(STARTS[b], SIZES[b])
            return remote(rows_ref.at[line], s["cot"].at[line], s["cot_sem"].at[0, b], s["cot_sem"].at[1, b], other_x)

        def out_copy(k):
            return remote(s["g_s"].at[k], s["o_r"].at[k], s["out_sem"].at[0, k], s["out_sem"].at[1, k], other_x)

        def right_copy(b):
            return remote(
                right.at[pl.ds(STARTS[b], SIZES[b])], right.at[pl.ds(tokens + STARTS[b], SIZES[b])],
                s["right1_sem"].at[0, b], s["right1_sem"].at[1, b], other_core,
            )

        def left_copy(k):
            low, z0 = spot(k)
            return remote(
                turned.at[:, low, pl.ds(z0, group), :, 1 - core],
                left.at[:, low, pl.ds(z0, group), :, :, pl.ds(tokens, tokens)],
                s["left1_sem"].at[0, k], s["left1_sem"].at[1, k], other_core,
            )

        ids_copy = remote(ids_ref, s["ids"], s["ids_sem"].at[0], s["ids_sem"].at[1], other_x)
        ids_copy.start()
        for b in range(BLOCKS):
            cot_copy(b).start()
        ids_copy.wait()
        ids = s["ids"][...]
        rows_of = lax.broadcasted_iota(jnp.int32, (rels, tokens), 0)
        onehot = jnp.where(rows_of == ids, 1.0, 0.0).T.astype(BF)
        table_copy.wait()
        for n in range(CHUNKS):
            part = slice(n * 2 * wide, (n + 1) * 2 * wide)
            s["rel"][:, part] = dot(onehot, s["table"][:, part]).astype(BF)
        for k in range(CHUNKS):
            w_copy(k).wait()
            w_copy(k + CHUNKS).wait()

        def columns(k):
            return slice(k * wide, (k + 1) * wide), slice(half + k * wide, half + (k + 1) * wide)

        def forward(b, k):
            re, im = columns(k)
            line = line_of(b)
            r_re, r_im = s["rel"][line, re].astype(F32), s["rel"][line, im].astype(F32)
            q_copy(b, k).wait_recv()
            q_re = s["q_r"][k, line, :wide].astype(F32)
            q_im = s["q_r"][k, line, wide:].astype(F32)
            z_re = (q_re * r_re - q_im * r_im).astype(BF)
            z_im = (q_re * r_im + q_im * r_re).astype(BF)
            s["mixed"][line, re] = z_re
            s["mixed"][line, im] = z_im
            for n in range(CHUNKS):
                part = slice(n * 2 * wide, (n + 1) * 2 * wide)
                term = dot(z_re, w[re, part]) + dot(z_im, w[im, part])
                s["pre"][line, part] = term if k == 0 else s["pre"][line, part] + term

        def activate(b):
            line = line_of(b)
            cot_copy(b).wait_recv()
            for n in range(CHUNKS):
                part = slice(n * 2 * wide, (n + 1) * 2 * wide)
                pre = s["pre"][line, part]
                sig = 1.0 / (1.0 + jnp.exp(-pre))
                slope = sig * (1.0 + pre * (1.0 - sig))
                right[line, part] = (s["cot"][line, part].astype(F32) * slope).astype(BF)
            right_copy(b).start()

        def back(b, k):
            re, im = columns(k)
            line = line_of(b)
            g_a = right[line]
            gz_re = dot_t(g_a, w[re])
            gz_im = dot_t(g_a, w[im])
            r_re, r_im = s["rel"][line, re].astype(F32), s["rel"][line, im].astype(F32)
            s["g_s"][k, line, :wide] = (gz_re * r_re + gz_im * r_im).astype(BF)
            s["g_s"][k, line, wide:] = (gz_im * r_re - gz_re * r_im).astype(BF)
            g_copy(b, k).start()
            q_re = s["q_r"][k, line, :wide].astype(F32)
            q_im = s["q_r"][k, line, wide:].astype(F32)
            s["pre"][line, re] = gz_re * q_re + gz_im * q_im
            s["pre"][line, im] = gz_im * q_re - gz_re * q_im

        def share(k):
            re, im = columns(k)
            low, z0 = spot(k)
            turn(k, s["mixed"][:, re], s["mixed"][:, im])
            left_copy(k).start()
            left[:, low, z0:z0 + group, :, :, 0:tokens] = turned[:, low, z0:z0 + group, :, core]

        for b in range(BLOCKS):
            for k in range(CHUNKS):
                forward(b, k)
                if b == BLOCKS - 1:
                    share(k)
            activate(b)
            for k in range(CHUNKS):
                back(b, k)
        for b in range(BLOCKS):
            right_copy(b).wait()
        for k in range(CHUNKS):
            left_copy(k).wait()

        swap = remote(s["rp_s"], s["rp_r"], s["rel_sem"].at[0, 3], s["rel_sem"].at[1, 3], other_core)
        aims = ((0, x, other_hop), (1, 1 - x, across), (2, 1 - x, other_x))

        def rel_start():
            row = lax.broadcasted_iota(jnp.int32, (rels, tokens), 0)
            side_of = lax.rem(row, 2)
            yy, zz = lax.rem(row // 2, NY), lax.rem(row // (2 * NY), NZ)
            hx = row // (2 * NY * NZ)
            base = (hx // NX) * (rels // 2) + ((yy * NZ + zz) * NX + lax.rem(hx, NX)) * NC
            who = s["ids"][...]

            def partial_for(which):
                match = jnp.where(base + which == who, 1.0, 0.0)
                total = None
                for side in range(2):
                    pick = jnp.where(side_of == side, match, 0.0).astype(BF)
                    values = s["pre"][:, side * half:(side + 1) * half]
                    head = values.astype(BF)
                    tail = (values - head.astype(F32)).astype(BF)
                    term = dot(pick, head) + dot(pick, tail)
                    total = term if total is None else total + term
                return total.reshape(2 * NX, NZ, 2 * NY, half)

            s["rp_s"][...] = partial_for(1 - core).astype(BF)
            swap.start()
            s["rp_o"][...] = partial_for(core)

        def rel_send(n):
            if n == 0:
                return remote(s["rel_s"].at[x], s["rel_r"].at[x], s["rel_sem"].at[0, 0], s["rel_sem"].at[1, x], other_hop)
            if n == 1:
                return remote(s["rel_s"].at[1 - x], s["rel_r"].at[x], s["rel_sem"].at[0, 1], s["rel_sem"].at[1, x], across)
            return remote(s["rel_s"].at[NX + 1 - x], s["rel_r"].at[0], s["rel_sem"].at[0, 2], s["rel_sem"].at[1, 2], other_x)

        def rel_join():
            swap.wait()
            for n in range(2 * NX):
                s["rel_s"][n] = (s["rp_o"][n] + s["rp_r"][n].astype(F32)).astype(BF)
            s["rp"][...] = s["rp_o"][NX + x] + s["rp_r"][NX + x].astype(F32)
            for n in range(3):
                rel_send(n).start()
            for k in range(CHUNKS):
                out_copy(k).start()

        def rel_take():
            rel_send(2).wait_recv()
            s["rp"][...] = s["rp"][...] + s["rel_r"][0].astype(F32)

        def x_copy(p, which):
            return remote(
                s["x_s"].at[which, p], s["x_r"].at[which, p],
                s["x_sem"].at[0, which, p], s["x_sem"].at[1, which, p], other_x,
            )

        def end(p, which, cols):
            def last(v):
                s["total"][which, p] = v.reshape(NX, 16, piece)
                s["x_s"][which, p] = s["total"][which, p, 1 - x].astype(BF)
                x_copy(p, which).start()

            def more():
                x_copy(p, which).wait_recv()
                wg_ref[:, cols] = (s["total"][which, p, x] + s["x_r"][which, p].astype(F32)) * scale

            return last, [more]

        streams, drains = [], []
        weight_rings("h1", left, right, NX * 16, streams, drains, end)
        streams.append((RELATION, [rel_start, rel_join, rel_take] + rel_tail(drains)))
        def settle_query():
            for k in range(CHUNKS):
                out_copy(k).wait_recv()
                for copy in out_parts("o_r", k):
                    copy.start()

        streams.append(((29.5,), [settle_query]))
        play(streams)
        write_grads()
        for b in range(BLOCKS):
            cot_copy(b).wait_send()
            for k in range(CHUNKS):
                g_copy(b, k).wait_send()
        for k in range(CHUNKS):
            out_copy(k).wait_send()
            for copy in out_parts("o_r", k):
                copy.wait()
        for drain in drains:
            drain()
        for n in range(3):
            rel_send(n).wait_send()
        for which in range(2):
            for p in range(PIECES):
                x_copy(p, which).wait_send()


def settle(wg_in, rg_in, qg_in, wg_out, rg_out, qg_out):
    wg_out[0] = wg_in[...]
    rg_out[...] = rg_in[...]
    qg_out[...] = qg_in[...]


def local(section_rows, weights, relation_table, relation_ids):
    tokens, width = section_rows.shape[1:]
    rels = relation_table.shape[0]
    total = tokens * lax.axis_size("batch")
    half = width // 2
    wide = half // CHUNKS
    piece = width // 2 // PIECES
    V = pltpu.VMEM
    D = pltpu.SemaphoreType.DMA
    chunks = (CHUNKS, tokens, 2 * wide)

    scratch = {
        "w": V((width, width), BF),
        "rows": V((tokens, width), BF),
        "wg": V((16, width), F32),
        "rg": V((1, width), F32),
        "table": V((rels, width), BF),
        "w_sem": D((2 * CHUNKS,)),
        "table_sem": D,
        "hop_sem": D((2, BLOCKS, CHUNKS)),
        "out_sem": D((2, CHUNKS)),
        "qg_sem": D((CHUNKS, 2)),
        "grad_sem": D((2,)),
        "rows_sem": D,
        "cot_sem": D((2, BLOCKS)),
        "ids_sem": D((2,)),
        "right0_sem": D((2, 3)),
        "right1_sem": D((2, BLOCKS)),
        "left0_sem": D((2, CHUNKS, 3)),
        "left1_sem": D((2, CHUNKS)),
        "rel_sem": D((2, 4)),
        "x_sem": D((2, 2, PIECES)),
        "q_s": V(chunks, BF),
        "q_r": V(chunks, BF),
        "g_s": V(chunks, BF),
        "g_r": V(chunks, BF),
        "o_r": V(chunks, BF),
        "cot": V((tokens, width), BF),
        "ids": V((1, tokens), jnp.int32),
        "rel": V((tokens, width), BF),
        "mixed": V((tokens, width), BF),
        "pre": V((tokens, width), F32),
        "turned": V((2, NY // 2, NZ, NX, NC, 16, tokens), BF),
        "left0": V((2, NY // 2, NZ, 16, 4 * tokens), BF),
        "right0": V((4 * tokens, width), BF),
        "left1": V((2, NY // 2, NZ, NX, 16, 2 * tokens), BF),
        "right1": V((2 * tokens, width), BF),
        "rp": V((NZ, 2 * NY, half), F32),
        "rp_o": V((2 * NX, NZ, 2 * NY, half), F32),
        "rp_s": V((2 * NX, NZ, 2 * NY, half), BF),
        "rp_r": V((2 * NX, NZ, 2 * NY, half), BF),
        "rel_s": V((2 * NX, NZ, 2 * NY, half), BF),
        "rel_r": V((NX, NZ, 2 * NY, half), BF),
        "rel_o": V((NY, 2, half), F32),
        "rel_i": V((NY - 1, 2, half), F32),
        "rel_y_sem": D((2, NY - 1)),
        "total": V((2, PIECES, NX, 16, piece), F32),
        "x_s": V((2, PIECES, 16, piece), BF),
        "x_r": V((2, PIECES, 16, piece), BF),
    }

    def ring_bufs(name, lead, n, rows, cols):
        h = n // 2
        for side in "sr":
            scratch[name + "_" + side + "f"] = V(lead + (2, rows, cols // 2), BF)
            scratch[name + "_" + side + "n"] = V(lead + (2, h - 1, rows, cols), BF)
            scratch[name + "_" + side + "s"] = D(lead + (2, h))

    for name, rows in (("h0", 16), ("h1", NX * 16)):
        ring_bufs(name + "_az", (PIECES,), NZ, NY * rows, piece)
        ring_bufs(name + "_ay", (PIECES,), NY, rows, piece)
        ring_bufs(name + "_by", (PIECES,), NY, NZ * rows, piece)
        ring_bufs(name + "_bz", (PIECES,), NZ, rows, piece)
        scratch[name + "_sum_z"] = V((NY, rows, half), F32)
        scratch[name + "_sum_y"] = V((NZ, rows, half), F32)
    ring_bufs("rz", (), NZ, 2 * NY, half)
    names = list(scratch)

    def body(*refs):
        kernel(total, *refs[:7], dict(zip(names, refs[7:])))

    vmem = pl.BlockSpec(memory_space=pltpu.VMEM)
    hbm = pl.BlockSpec(memory_space=pl.ANY)
    wg, rg, qg = pl.pallas_call(
        body,
        out_shape=(
            jax.ShapeDtypeStruct((16, width), F32),
            jax.ShapeDtypeStruct((1, width), F32),
            jax.ShapeDtypeStruct((tokens, width), BF),
        ),
        in_specs=[hbm, hbm, hbm, vmem],
        out_specs=(hbm, hbm, hbm),
        scratch_shapes=[scratch[n] for n in names],
        compiler_params=pltpu.CompilerParams(
            collective_id=0, has_side_effects=True, vmem_limit_bytes=60 * 1024 * 1024
        ),
        name="backward",
    )(section_rows[0], weights[0], relation_table, relation_ids.reshape(1, tokens))
    shapes = (
        jax.ShapeDtypeStruct((1, 16, width), F32),
        jax.ShapeDtypeStruct((1, width), F32),
        jax.ShapeDtypeStruct((tokens, width), BF),
    )
    return pl.pallas_call(
        settle, out_shape=shapes, in_specs=[vmem] * 3, out_specs=(vmem, vmem, vmem), name="settle"
    )(wg, rg, qg)


def solution(mesh):
    return jax.shard_map(
        local,
        mesh=mesh,
        in_specs=(P("hop", "batch", None), P("hop", None, None), P(), P("batch")),
        out_specs=(P("hop", "batch", None), P(("hop", "batch"), None), P("batch", None)),
        check_vma=False,
    )
```

```python
import functools
import math

import jax
import jax.numpy as jnp
from jax import lax
from jax.experimental import pallas as pl
from jax.experimental.pallas import tpu as pltpu
from jax.sharding import PartitionSpec as P

MESH = pl.DeviceIdType.MESH
BF = jnp.bfloat16
F32 = jnp.float32
NY, NZ, NX, NC = 4, 8, 2, 2
CHUNKS = 4
PIECES = 2
SIZES = (64, 64)
BLOCKS = len(SIZES)
STARTS = tuple(sum(SIZES[:n]) for n in range(BLOCKS))
Z_FIRST = (0, 4, 10, 16, 22, 22.5, 26, 29, 32)
Y_FIRST = (0, 7, 19, 19.5, 23.4, 27.5, 31)
RELATION = (1.5, 5.5, 14.5, 14.6, 18.1, 21.1, 24.1, 27.1, 31.1)


def dot(a, b):
    return jnp.dot(a, b, preferred_element_type=F32)


def dot_t(a, b):
    return lax.dot_general(a, b, (((1,), (1,)), ((), ())), preferred_element_type=F32)


def remote(src, dst, send, recv, device):
    return pltpu.make_async_remote_copy(
        src_ref=src, dst_ref=dst, send_sem=send, recv_sem=recv,
        device_id=device, device_id_type=MESH,
    )


def ring(n, index, own, send_far, send_near, recv_far, recv_near, ssem, rsem, devices, finish):
    half = n // 2
    cut = send_far.shape[-1]

    def copy(way, step):
        src = send_far.at[way] if step == 1 else send_near.at[way, step - 2]
        dst = recv_far.at[way] if step == 1 else recv_near.at[way, step - 2]
        return remote(src, dst, ssem.at[way, step - 1], rsem.at[way, step - 1], devices[way])

    def first():
        block = own(lax.rem(index + half, n)).astype(BF)
        send_far[0] = block[:, :cut]
        copy(0, 1).start()
        send_far[1] = block[:, cut:]
        copy(1, 1).start()

    def middle(step):
        distance = half + 1 - step
        for way in (0, 1):
            target = lax.rem(index + (distance if way == 0 else n - distance), n)
            block = own(target)
            copy(way, step - 1).wait_recv()
            if step == 2:
                got = recv_far[way].astype(F32)
                low, high = block[:, :cut], block[:, cut:]
                low, high = (low + got, high) if way == 0 else (low, high + got)
                send_near[way, 0, :, :cut] = low.astype(BF)
                send_near[way, 0, :, cut:] = high.astype(BF)
            else:
                got = recv_near[way, step - 3].astype(F32)
                send_near[way, step - 2] = (block + got).astype(BF)
            copy(way, step).start()

    def last():
        block = own(index)
        copy(0, half).wait_recv()
        copy(1, half).wait_recv()
        finish(block + recv_near[0, half - 2].astype(F32) + recv_near[1, half - 2].astype(F32))

    def drain():
        for step in range(1, half + 1):
            for way in (0, 1):
                copy(way, step).wait_send()

    return [first] + [functools.partial(middle, t) for t in range(2, half + 1)] + [last], drain


def ring_of_eight(index, own, sends, recvs, ssem, rsem, one_away, two_away, finish):
    n = 8
    pair_s, far_s, near_s = sends
    pair_r, far_r, near_r = recvs
    cut = far_s.shape[-1]

    def copy(way, kind):
        src, dst = ((pair_s, pair_r), (far_s, far_r), (near_s, near_r))[kind]
        device = (one_away if kind == 0 else two_away)[way]
        return remote(src.at[way], dst.at[way], ssem.at[way, kind], rsem.at[way, kind], device)

    def place(way, distance):
        return lax.rem(index + (distance if way == 0 else n - distance), n)

    def first():
        block = own(lax.rem(index + 4, n)).astype(BF)
        for way in (0, 1):
            pair_s[way, 0] = own(place(way, 3)).astype(BF)
            pair_s[way, 1] = own(place(way, 1)).astype(BF)
            far_s[way] = block[:, :cut] if way == 0 else block[:, cut:]
            copy(way, 1).start()
            copy(way, 0).start()

    def middle():
        for way in (0, 1):
            block = own(place(way, 2))
            copy(way, 0).wait_recv()
            copy(way, 1).wait_recv()
            block = block + pair_r[way, 0].astype(F32)
            got = far_r[way].astype(F32)
            low, high = block[:, :cut], block[:, cut:]
            low, high = (low + got, high) if way == 0 else (low, high + got)
            near_s[way, :, :cut] = low.astype(BF)
            near_s[way, :, cut:] = high.astype(BF)
            copy(way, 2).start()

    def last():
        block = own(index) + pair_r[0, 1].astype(F32) + pair_r[1, 1].astype(F32)
        copy(0, 2).wait_recv()
        copy(1, 2).wait_recv()
        finish(block + near_r[0].astype(F32) + near_r[1].astype(F32))

    def drain():
        for way in (0, 1):
            for kind in range(3):
                copy(way, kind).wait_send()

    return [first, middle, last], drain


def play(streams):
    events = []
    for times, steps in streams:
        events += [(t, len(events) + n, step) for n, (t, step) in enumerate(zip(times, steps))]
    for _, _, step in sorted(events, key=lambda e: e[:2]):
        step()


def kernel(rows_total, rows_hbm, w_ref, table_ref, ids_ref, wg_hbm, rg_hbm, qg_hbm, s):
    hop = lax.axis_index("hop")
    place = lax.axis_index("batch")
    core = lax.rem(place, NC)
    x = lax.rem(place // NC, NX)
    z = lax.rem(place // (NC * NX), NZ)
    y = place // (NC * NX * NZ)

    def at(h, yy, zz, xx, cc):
        return (h, ((yy * NZ + zz) * NX + xx) * NC + cc)

    other_core = at(hop, y, z, x, 1 - core)
    other_hop = at(1 - hop, y, z, x, core)
    other_x = at(hop, y, z, 1 - x, core)
    diagonal = at(hop, y, z, 1 - x, 1 - core)
    across = at(1 - hop, y, z, 1 - x, core)
    y_ways = (at(hop, lax.rem(y + 1, NY), z, x, core), at(hop, lax.rem(y + NY - 1, NY), z, x, core))
    z_ways = (at(hop, y, lax.rem(z + 1, NZ), x, core), at(hop, y, lax.rem(z + NZ - 1, NZ), x, core))

    rows_ref, wg_ref, rg_ref = s["rows"], s["wg"], s["rg"]
    tokens, width = rows_ref.shape
    half = width // 2
    wide = half // CHUNKS
    rels = table_ref.shape[0]
    colour = width // 2
    piece = colour // PIECES
    group = NZ * (NY // 2) // CHUNKS

    def w_copy(j):
        part = pl.ds(j * wide, wide)
        return pltpu.make_async_copy(w_ref.at[part], s["w"].at[part], s["w_sem"].at[j])

    table_copy = pltpu.make_async_copy(table_ref, s["table"], s["table_sem"])
    rows_copy = pltpu.make_async_copy(rows_hbm, rows_ref, s["rows_sem"])
    rows_copy.start()
    w_copy(0).start()
    w_copy(CHUNKS).start()

    y_far = at(hop, lax.rem(y + NY // 2, NY), z, x, core)
    z_two = (at(hop, y, lax.rem(z + 2, NZ), x, core), at(hop, y, lax.rem(z + NZ - 2, NZ), x, core))
    partners = (other_core, other_hop, other_x, diagonal, across, y_far) + y_ways + z_ways + z_two
    barrier = pltpu.get_barrier_semaphore()
    for device in partners:
        pl.semaphore_signal(barrier, inc=1, device_id=device, device_id_type=MESH)

    def lead(k):
        for part in range(2):
            w_copy(k + part * CHUNKS).wait()
            weight = s["w"][pl.ds(part * half + k * wide, wide)]
            s["q_s"][k, :, part * wide:(part + 1) * wide] = dot_t(rows_ref[...], weight).astype(BF)

    for k in range(1, CHUNKS):
        w_copy(k).start()
        w_copy(k + CHUNKS).start()
    table_copy.start()
    rows_copy.wait()
    pl.when(hop == 0)(lambda: lead(0))
    pl.semaphore_wait(barrier, len(partners))

    w, turned = s["w"], s["turned"]

    def hop_copy(src, dst, b, k):
        line = pl.ds(STARTS[b], SIZES[b])
        return remote(
            s[src].at[k, line], s[dst].at[k, line], s["hop_sem"].at[0, b, k], s["hop_sem"].at[1, b, k], across
        )

    def line_of(b):
        return slice(STARTS[b], STARTS[b] + SIZES[b])

    def out_parts(src, k):
        return [
            pltpu.make_async_copy(
                s[src].at[k, :, pl.ds(part * wide, wide)],
                qg_hbm.at[:, pl.ds(part * half + k * wide, wide)],
                s["qg_sem"].at[k, part],
            )
            for part in range(2)
        ]

    def write_grads():
        pairs = ((wg_ref, wg_hbm, 0), (rg_ref, rg_hbm, 1))
        copies = [pltpu.make_async_copy(src, dst, s["grad_sem"].at[n]) for src, dst, n in pairs]
        for copy in copies:
            copy.start()
        for copy in copies:
            copy.wait()

    def q_copy(b, k):
        return hop_copy("q_s", "q_r", b, k)

    def g_copy(b, k):
        return hop_copy("g_s", "g_r", b, k)

    def spot(k):
        return k // (CHUNKS // 2), k % (CHUNKS // 2) * group

    def turn(k, re, im):
        low, z0 = spot(k)
        for part, values in enumerate((re, im)):
            flat = values.astype(F32).T.astype(BF)
            for g in range(group):
                for xx in range(NX):
                    for cc in range(NC):
                        row = ((g * NX + xx) * NC + cc) * 16
                        turned[part, low, z0 + g, xx, cc] = flat[row:row + 16]

    def bufs(name):
        return [s[name + "_" + b] for b in ("sf", "sn", "rf", "rn", "ss", "rs")]

    def sub(refs, p):
        return [r.at[p] for r in refs]

    def weight_rings(name, left, right, rows, streams, drains, end):
        depth = right.shape[0]

        def by_z(cols):
            def own(zz):
                a = left[:, :, zz].reshape(NY * rows, depth)
                return dot(a, right[:, cols])
            return own

        def by_y(cols):
            def own(yy):
                a = left[yy // 2, lax.rem(yy, 2)].reshape(NZ * rows, depth)
                return dot(a, right[:, cols])
            return own

        for p in range(PIECES):
            here = slice(p * piece, (p + 1) * piece)
            cols = (here, slice(colour + p * piece, colour + (p + 1) * piece))

            def keep_z(v, here=here):
                s[name + "_sum_z"][:, :, here] = v.reshape(NY, rows, piece)

            def keep_y(v, here=here):
                s[name + "_sum_y"][:, :, here] = v.reshape(NZ, rows, piece)

            def from_z(yy, here=here):
                return s[name + "_sum_z"][yy, :, here]

            def from_y(zz, here=here):
                return s[name + "_sum_y"][zz, :, here]

            last_z, more_z = end(p, 0, cols[0])
            last_y, more_y = end(p, 1, cols[1])
            one = ring(NZ, z, by_z(cols[0]), *sub(bufs(name + "_az"), p), z_ways, keep_z)
            two = ring(NY, y, from_z, *sub(bufs(name + "_ay"), p), y_ways, last_z)
            three = ring(NY, y, by_y(cols[1]), *sub(bufs(name + "_by"), p), y_ways, keep_y)
            refs = {b: s[name + "_bz_" + b].at[p] for b in ("sp", "sf", "sn", "rp", "rf", "rn", "ss", "rs")}
            four = ring_of_eight(
                z, from_y, [refs[b] for b in ("sp", "sf", "sn")], [refs[b] for b in ("rp", "rf", "rn")],
                refs["ss"], refs["rs"], z_ways, z_two, last_y,
            )
            streams.append(([t + 0.5 * p for t in Z_FIRST], one[0] + two[0] + more_z))
            streams.append(([t + 0.5 * p + 0.25 for t in Y_FIRST], three[0] + four[0] + more_y))
            drains += [one[1], two[1], three[1], four[1]]

    scale = 1.0 / math.sqrt(rows_total)
    rel_scale = math.sqrt(rels / rows_total)

    def rel_copy(src, slot, sem, device):
        return remote(s["rel_s"].at[src], s["rel_r"].at[slot], s["rel_sem"].at[0, sem], s["rel_sem"].at[1, sem], device)

    def rel_y_copy(n):
        target = lax.rem(y + n, NY)
        return remote(
            s["rel_o"].at[target], s["rel_i"].at[n - 1], s["rel_y_sem"].at[0, n - 1], s["rel_y_sem"].at[1, n - 1],
            (y_ways[0], y_far, y_ways[1])[n - 1],
        )

    def rel_tail(drains):
        def own(zz):
            return s["rp"][zz]

        def split(v):
            for yy in range(NY):
                for side in range(2):
                    s["rel_o"][yy, side:side + 1] = v[yy * 2 + side:yy * 2 + side + 1]
            for n in range(1, NY):
                rel_y_copy(n).start()

        def final():
            for n in range(1, NY):
                rel_y_copy(n).wait_recv()
            total = s["rel_o"][y] + s["rel_i"][0] + s["rel_i"][1] + s["rel_i"][2]
            rg_ref[:, :half] = total[0:1] * rel_scale
            rg_ref[:, half:] = total[1:2] * rel_scale

        steps, drain = ring(NZ, z, own, *bufs("rz"), z_ways, split)
        drains.append(drain)
        drains.append(lambda: [rel_y_copy(n).wait_send() for n in range(1, NY)])
        return steps + [final]

    @pl.when(hop == 0)
    def _():
        left, right = s["left0"], s["right0"]
        dest = (None, other_core, other_x, diagonal)

        def slot(n):
            return right.at[pl.ds(n * tokens, tokens)]

        sends = s["right0_sem"]
        to_core = remote(rows_ref, slot(1), sends.at[0, 0], sends.at[1, 0], other_core)
        to_x = remote(rows_ref, slot(2), sends.at[0, 1], sends.at[1, 1], other_x)
        onward = remote(slot(2), slot(3), sends.at[0, 2], sends.at[1, 2], other_core)
        to_x.start()

        for k in range(CHUNKS):
            if k:
                lead(k)
            q_copy(0, k).start()
        for b in range(1, BLOCKS):
            for k in range(CHUNKS):
                q_copy(b, k).start()
        to_core.start()
        right[0:tokens] = rows_ref[...]
        table_copy.wait()

        def left_copy(k, n):
            low, z0 = spot(k)
            xx, cc = (x, 1 - core) if n == 1 else (1 - x, core if n == 2 else 1 - core)
            return remote(
                turned.at[:, low, pl.ds(z0, group), xx, cc],
                left.at[:, low, pl.ds(z0, group), :, pl.ds(n * tokens, tokens)],
                s["left0_sem"].at[0, k, n - 1], s["left0_sem"].at[1, k, n - 1], dest[n],
            )

        for b in range(BLOCKS):
            for k in range(CHUNKS):
                g_copy(b, k).wait_recv()
                if b == BLOCKS - 1:
                    low, z0 = spot(k)
                    turn(k, s["g_r"][k, :, :wide], s["g_r"][k, :, wide:])
                    for n in (2, 3, 1):
                        left_copy(k, n).start()
                    left[:, low, z0:z0 + group, :, 0:tokens] = turned[:, low, z0:z0 + group, x, core]
                    for copy in out_parts("g_r", k):
                        copy.start()
            if b == 0:
                to_x.wait_recv()
                onward.start()
        to_core.wait()
        to_x.wait_send()
        onward.wait()
        for k in range(CHUNKS):
            for n in (1, 2, 3):
                left_copy(k, n).wait()

        streams, drains = [], []

        def end(p, which, cols):
            def last(v):
                wg_ref[:, cols] = v * scale
            return last, []

        def rel_take():
            for slot in range(NX):
                rel_copy(0, slot, slot, across).wait_recv()
            s["rp"][...] = s["rel_r"][0].astype(F32) + s["rel_r"][1].astype(F32)

        weight_rings("h0", left, right, 16, streams, drains, end)
        streams.append((RELATION[2:], [rel_take] + rel_tail(drains)))
        play(streams)
        write_grads()
        for k in range(CHUNKS):
            for b in range(BLOCKS):
                q_copy(b, k).wait_send()
            for copy in out_parts("g_r", k):
                copy.wait()
        for drain in drains:
            drain()

    @pl.when(hop == 1)
    def _():
        left, right = s["left1"], s["right1"]

        def cot_copy(b):
            line = pl.ds(STARTS[b], SIZES[b])
            return remote(rows_ref.at[line], s["cot"].at[line], s["cot_sem"].at[0, b], s["cot_sem"].at[1, b], other_x)

        def out_copy(k):
            return remote(s["g_s"].at[k], s["o_r"].at[k], s["out_sem"].at[0, k], s["out_sem"].at[1, k], other_x)

        def right_copy(b):
            return remote(
                right.at[pl.ds(STARTS[b], SIZES[b])], right.at[pl.ds(tokens + STARTS[b], SIZES[b])],
                s["right1_sem"].at[0, b], s["right1_sem"].at[1, b], other_core,
            )

        def left_copy(k):
            low, z0 = spot(k)
            return remote(
                turned.at[:, low, pl.ds(z0, group), :, 1 - core],
                left.at[:, low, pl.ds(z0, group), :, :, pl.ds(tokens, tokens)],
                s["left1_sem"].at[0, k], s["left1_sem"].at[1, k], other_core,
            )

        ids_copy = remote(ids_ref, s["ids"], s["ids_sem"].at[0], s["ids_sem"].at[1], other_x)
        ids_copy.start()
        for b in range(BLOCKS):
            cot_copy(b).start()
        ids_copy.wait()
        ids = s["ids"][...]
        rows_of = lax.broadcasted_iota(jnp.int32, (rels, tokens), 0)
        onehot = jnp.where(rows_of == ids, 1.0, 0.0).T.astype(BF)
        table_copy.wait()
        for n in range(CHUNKS):
            part = slice(n * 2 * wide, (n + 1) * 2 * wide)
            s["rel"][:, part] = dot(onehot, s["table"][:, part]).astype(BF)
        for k in range(CHUNKS):
            w_copy(k).wait()
            w_copy(k + CHUNKS).wait()

        def columns(k):
            return slice(k * wide, (k + 1) * wide), slice(half + k * wide, half + (k + 1) * wide)

        def forward(b, k):
            re, im = columns(k)
            line = line_of(b)
            r_re, r_im = s["rel"][line, re].astype(F32), s["rel"][line, im].astype(F32)
            q_copy(b, k).wait_recv()
            q_re = s["q_r"][k, line, :wide].astype(F32)
            q_im = s["q_r"][k, line, wide:].astype(F32)
            z_re = (q_re * r_re - q_im * r_im).astype(BF)
            z_im = (q_re * r_im + q_im * r_re).astype(BF)
            s["mixed"][line, re] = z_re
            s["mixed"][line, im] = z_im
            for n in range(CHUNKS):
                part = slice(n * 2 * wide, (n + 1) * 2 * wide)
                term = dot(z_re, w[re, part]) + dot(z_im, w[im, part])
                s["pre"][line, part] = term if k == 0 else s["pre"][line, part] + term

        def activate(b):
            line = line_of(b)
            cot_copy(b).wait_recv()
            for n in range(CHUNKS):
                part = slice(n * 2 * wide, (n + 1) * 2 * wide)
                pre = s["pre"][line, part]
                sig = 1.0 / (1.0 + jnp.exp(-pre))
                slope = sig * (1.0 + pre * (1.0 - sig))
                right[line, part] = (s["cot"][line, part].astype(F32) * slope).astype(BF)
            right_copy(b).start()

        def back(b, k):
            re, im = columns(k)
            line = line_of(b)
            g_a = right[line]
            gz_re = dot_t(g_a, w[re])
            gz_im = dot_t(g_a, w[im])
            r_re, r_im = s["rel"][line, re].astype(F32), s["rel"][line, im].astype(F32)
            s["g_s"][k, line, :wide] = (gz_re * r_re + gz_im * r_im).astype(BF)
            s["g_s"][k, line, wide:] = (gz_im * r_re - gz_re * r_im).astype(BF)
            g_copy(b, k).start()
            q_re = s["q_r"][k, line, :wide].astype(F32)
            q_im = s["q_r"][k, line, wide:].astype(F32)
            s["pre"][line, re] = gz_re * q_re + gz_im * q_im
            s["pre"][line, im] = gz_im * q_re - gz_re * q_im

        def share(k):
            re, im = columns(k)
            low, z0 = spot(k)
            turn(k, s["mixed"][:, re], s["mixed"][:, im])
            left_copy(k).start()
            left[:, low, z0:z0 + group, :, :, 0:tokens] = turned[:, low, z0:z0 + group, :, core]

        for b in range(BLOCKS):
            for k in range(CHUNKS):
                forward(b, k)
                if b == BLOCKS - 1:
                    share(k)
            activate(b)
            for k in range(CHUNKS):
                back(b, k)
        for b in range(BLOCKS):
            right_copy(b).wait()
        for k in range(CHUNKS):
            left_copy(k).wait()

        swap = remote(s["rp_s"], s["rp_r"], s["rel_sem"].at[0, 3], s["rel_sem"].at[1, 3], other_core)
        aims = ((0, x, other_hop), (1, 1 - x, across), (2, 1 - x, other_x))

        def rel_start():
            row = lax.broadcasted_iota(jnp.int32, (rels, tokens), 0)
            side_of = lax.rem(row, 2)
            yy, zz = lax.rem(row // 2, NY), lax.rem(row // (2 * NY), NZ)
            hx = row // (2 * NY * NZ)
            base = (hx // NX) * (rels // 2) + ((yy * NZ + zz) * NX + lax.rem(hx, NX)) * NC
            who = s["ids"][...]

            def partial_for(which):
                match = jnp.where(base + which == who, 1.0, 0.0)
                total = None
                for side in range(2):
                    pick = jnp.where(side_of == side, match, 0.0).astype(BF)
                    values = s["pre"][:, side * half:(side + 1) * half]
                    head = values.astype(BF)
                    tail = (values - head.astype(F32)).astype(BF)
                    term = dot(pick, head) + dot(pick, tail)
                    total = term if total is None else total + term
                return total.reshape(2 * NX, NZ, 2 * NY, half)

            s["rp_s"][...] = partial_for(1 - core).astype(BF)
            swap.start()
            s["rp_o"][...] = partial_for(core)

        def rel_send(n):
            if n == 0:
                return remote(s["rel_s"].at[x], s["rel_r"].at[x], s["rel_sem"].at[0, 0], s["rel_sem"].at[1, x], other_hop)
            if n == 1:
                return remote(s["rel_s"].at[1 - x], s["rel_r"].at[x], s["rel_sem"].at[0, 1], s["rel_sem"].at[1, x], across)
            return remote(s["rel_s"].at[NX + 1 - x], s["rel_r"].at[0], s["rel_sem"].at[0, 2], s["rel_sem"].at[1, 2], other_x)

        def rel_join():
            swap.wait()
            for n in range(2 * NX):
                s["rel_s"][n] = (s["rp_o"][n] + s["rp_r"][n].astype(F32)).astype(BF)
            s["rp"][...] = s["rp_o"][NX + x] + s["rp_r"][NX + x].astype(F32)
            for n in range(3):
                rel_send(n).start()
            for k in range(CHUNKS):
                out_copy(k).start()

        def rel_take():
            rel_send(2).wait_recv()
            s["rp"][...] = s["rp"][...] + s["rel_r"][0].astype(F32)

        def x_copy(p, which):
            return remote(
                s["x_s"].at[which, p], s["x_r"].at[which, p],
                s["x_sem"].at[0, which, p], s["x_sem"].at[1, which, p], other_x,
            )

        def end(p, which, cols):
            def last(v):
                s["total"][which, p] = v.reshape(NX, 16, piece)
                s["x_s"][which, p] = s["total"][which, p, 1 - x].astype(BF)
                x_copy(p, which).start()

            def more():
                x_copy(p, which).wait_recv()
                wg_ref[:, cols] = (s["total"][which, p, x] + s["x_r"][which, p].astype(F32)) * scale

            return last, [more]

        streams, drains = [], []
        weight_rings("h1", left, right, NX * 16, streams, drains, end)
        streams.append((RELATION, [rel_start, rel_join, rel_take] + rel_tail(drains)))
        def settle_query():
            for k in range(CHUNKS):
                out_copy(k).wait_recv()
                for copy in out_parts("o_r", k):
                    copy.start()

        streams.append(((29.5,), [settle_query]))
        play(streams)
        write_grads()
        for b in range(BLOCKS):
            cot_copy(b).wait_send()
            for k in range(CHUNKS):
                g_copy(b, k).wait_send()
        for k in range(CHUNKS):
            out_copy(k).wait_send()
            for copy in out_parts("o_r", k):
                copy.wait()
        for drain in drains:
            drain()
        for n in range(3):
            rel_send(n).wait_send()
        for which in range(2):
            for p in range(PIECES):
                x_copy(p, which).wait_send()


def settle(wg_in, rg_in, qg_in, wg_out, rg_out, qg_out):
    wg_out[0] = wg_in[...]
    rg_out[...] = rg_in[...]
    qg_out[...] = qg_in[...]


def local(section_rows, weights, relation_table, relation_ids):
    tokens, width = section_rows.shape[1:]
    rels = relation_table.shape[0]
    total = tokens * lax.axis_size("batch")
    half = width // 2
    wide = half // CHUNKS
    piece = width // 2 // PIECES
    V = pltpu.VMEM
    D = pltpu.SemaphoreType.DMA
    chunks = (CHUNKS, tokens, 2 * wide)

    scratch = {
        "w": V((width, width), BF),
        "rows": V((tokens, width), BF),
        "wg": V((16, width), F32),
        "rg": V((1, width), F32),
        "table": V((rels, width), BF),
        "w_sem": D((2 * CHUNKS,)),
        "table_sem": D,
        "hop_sem": D((2, BLOCKS, CHUNKS)),
        "out_sem": D((2, CHUNKS)),
        "qg_sem": D((CHUNKS, 2)),
        "grad_sem": D((2,)),
        "rows_sem": D,
        "cot_sem": D((2, BLOCKS)),
        "ids_sem": D((2,)),
        "right0_sem": D((2, 3)),
        "right1_sem": D((2, BLOCKS)),
        "left0_sem": D((2, CHUNKS, 3)),
        "left1_sem": D((2, CHUNKS)),
        "rel_sem": D((2, 4)),
        "x_sem": D((2, 2, PIECES)),
        "q_s": V(chunks, BF),
        "q_r": V(chunks, BF),
        "g_s": V(chunks, BF),
        "g_r": V(chunks, BF),
        "o_r": V(chunks, BF),
        "cot": V((tokens, width), BF),
        "ids": V((1, tokens), jnp.int32),
        "rel": V((tokens, width), BF),
        "mixed": V((tokens, width), BF),
        "pre": V((tokens, width), F32),
        "turned": V((2, NY // 2, NZ, NX, NC, 16, tokens), BF),
        "left0": V((2, NY // 2, NZ, 16, 4 * tokens), BF),
        "right0": V((4 * tokens, width), BF),
        "left1": V((2, NY // 2, NZ, NX, 16, 2 * tokens), BF),
        "right1": V((2 * tokens, width), BF),
        "rp": V((NZ, 2 * NY, half), F32),
        "rp_o": V((2 * NX, NZ, 2 * NY, half), F32),
        "rp_s": V((2 * NX, NZ, 2 * NY, half), BF),
        "rp_r": V((2 * NX, NZ, 2 * NY, half), BF),
        "rel_s": V((2 * NX, NZ, 2 * NY, half), BF),
        "rel_r": V((NX, NZ, 2 * NY, half), BF),
        "rel_o": V((NY, 2, half), F32),
        "rel_i": V((NY - 1, 2, half), F32),
        "rel_y_sem": D((2, NY - 1)),
        "total": V((2, PIECES, NX, 16, piece), F32),
        "x_s": V((2, PIECES, 16, piece), BF),
        "x_r": V((2, PIECES, 16, piece), BF),
    }

    def ring_bufs(name, lead, n, rows, cols):
        h = n // 2
        for side in "sr":
            scratch[name + "_" + side + "f"] = V(lead + (2, rows, cols // 2), BF)
            scratch[name + "_" + side + "n"] = V(lead + (2, h - 1, rows, cols), BF)
            scratch[name + "_" + side + "s"] = D(lead + (2, h))

    for name, rows in (("h0", 16), ("h1", NX * 16)):
        ring_bufs(name + "_az", (PIECES,), NZ, NY * rows, piece)
        ring_bufs(name + "_ay", (PIECES,), NY, rows, piece)
        ring_bufs(name + "_by", (PIECES,), NY, NZ * rows, piece)
        for side in "sr":
            scratch[name + "_bz_" + side + "p"] = V((PIECES, 2, 2, rows, piece), BF)
            scratch[name + "_bz_" + side + "f"] = V((PIECES, 2, rows, piece // 2), BF)
            scratch[name + "_bz_" + side + "n"] = V((PIECES, 2, rows, piece), BF)
            scratch[name + "_bz_" + side + "s"] = D((PIECES, 2, 3))
        scratch[name + "_sum_z"] = V((NY, rows, half), F32)
        scratch[name + "_sum_y"] = V((NZ, rows, half), F32)
    ring_bufs("rz", (), NZ, 2 * NY, half)
    names = list(scratch)

    def body(*refs):
        kernel(total, *refs[:7], dict(zip(names, refs[7:])))

    vmem = pl.BlockSpec(memory_space=pltpu.VMEM)
    hbm = pl.BlockSpec(memory_space=pl.ANY)
    wg, rg, qg = pl.pallas_call(
        body,
        out_shape=(
            jax.ShapeDtypeStruct((16, width), F32),
            jax.ShapeDtypeStruct((1, width), F32),
            jax.ShapeDtypeStruct((tokens, width), BF),
        ),
        in_specs=[hbm, hbm, hbm, vmem],
        out_specs=(hbm, hbm, hbm),
        scratch_shapes=[scratch[n] for n in names],
        compiler_params=pltpu.CompilerParams(
            collective_id=0, has_side_effects=True, vmem_limit_bytes=60 * 1024 * 1024
        ),
        name="backward",
    )(section_rows[0], weights[0], relation_table, relation_ids.reshape(1, tokens))
    shapes = (
        jax.ShapeDtypeStruct((1, 16, width), F32),
        jax.ShapeDtypeStruct((1, width), F32),
        jax.ShapeDtypeStruct((tokens, width), BF),
    )
    return pl.pallas_call(
        settle, out_shape=shapes, in_specs=[vmem] * 3, out_specs=(vmem, vmem, vmem), name="settle"
    )(wg, rg, qg)


def solution(mesh):
    return jax.shard_map(
        local,
        mesh=mesh,
        in_specs=(P("hop", "batch", None), P("hop", None, None), P(), P("batch")),
        out_specs=(P("hop", "batch", None), P(("hop", "batch"), None), P("batch", None)),
        check_vma=False,
    )
```

```python
import functools
import math
import types

import jax
import jax.numpy as jnp
from jax import lax
from jax.experimental import pallas as pl
from jax.experimental.pallas import tpu as pltpu
from jax.sharding import PartitionSpec as P

MESH = pl.DeviceIdType.MESH
BF = jnp.bfloat16
F32 = jnp.float32
NY, NZ, NX, NC = 4, 8, 2, 2
CHUNKS = 4
PIECES = 2
SIZES = (64, 64)
BLOCKS = len(SIZES)
STARTS = tuple(sum(SIZES[:n]) for n in range(BLOCKS))
Z_FIRST = (0, 4, 10, 16, 22, 22.5, 26.5, 30)
Y_FIRST = (0, 7, 19, 19.5, 23.4, 27.5, 31)
RELATION = (1.5, 5.5, 14.5, 14.6, 18.1, 21.1, 24.1, 27.1, 31.1)


def dot(a, b):
    return jnp.dot(a, b, preferred_element_type=F32)


def dot_t(a, b):
    return lax.dot_general(a, b, (((1,), (1,)), ((), ())), preferred_element_type=F32)


def remote(src, dst, send, recv, device):
    return pltpu.make_async_remote_copy(
        src_ref=src, dst_ref=dst, send_sem=send, recv_sem=recv,
        device_id=device, device_id_type=MESH,
    )


def ring(n, index, own, send_far, send_near, recv_far, recv_near, ssem, rsem, devices, finish):
    half = n // 2
    cut = send_far.shape[-1]

    def copy(way, step):
        src = send_far.at[way] if step == 1 else send_near.at[way, step - 2]
        dst = recv_far.at[way] if step == 1 else recv_near.at[way, step - 2]
        return remote(src, dst, ssem.at[way, step - 1], rsem.at[way, step - 1], devices[way])

    def first():
        block = own(lax.rem(index + half, n)).astype(BF)
        send_far[0] = block[:, :cut]
        copy(0, 1).start()
        send_far[1] = block[:, cut:]
        copy(1, 1).start()

    def middle(step):
        distance = half + 1 - step
        for way in (0, 1):
            target = lax.rem(index + (distance if way == 0 else n - distance), n)
            block = own(target)
            copy(way, step - 1).wait_recv()
            if step == 2:
                got = recv_far[way].astype(F32)
                low, high = block[:, :cut], block[:, cut:]
                low, high = (low + got, high) if way == 0 else (low, high + got)
                send_near[way, 0, :, :cut] = low.astype(BF)
                send_near[way, 0, :, cut:] = high.astype(BF)
            else:
                got = recv_near[way, step - 3].astype(F32)
                send_near[way, step - 2] = (block + got).astype(BF)
            copy(way, step).start()

    def last():
        block = own(index)
        copy(0, half).wait_recv()
        copy(1, half).wait_recv()
        finish(block + recv_near[0, half - 2].astype(F32) + recv_near[1, half - 2].astype(F32))

    def drain():
        for step in range(1, half + 1):
            for way in (0, 1):
                copy(way, step).wait_send()

    return [first] + [functools.partial(middle, t) for t in range(2, half + 1)] + [last], drain


def ring_of_eight(index, own, sends, recvs, ssem, rsem, one_away, two_away, finish):
    n = 8
    pair_s, far_s, near_s = sends
    pair_r, far_r, near_r = recvs
    cut = far_s.shape[-1]

    def copy(way, kind):
        src, dst = ((pair_s, pair_r), (far_s, far_r), (near_s, near_r))[kind]
        device = (one_away if kind == 0 else two_away)[way]
        return remote(src.at[way], dst.at[way], ssem.at[way, kind], rsem.at[way, kind], device)

    def place(way, distance):
        return lax.rem(index + (distance if way == 0 else n - distance), n)

    def first():
        block = own(lax.rem(index + 4, n)).astype(BF)
        for way in (0, 1):
            pair_s[way, 0] = own(place(way, 3)).astype(BF)
            pair_s[way, 1] = own(place(way, 1)).astype(BF)
            far_s[way] = block[:, :cut] if way == 0 else block[:, cut:]
            copy(way, 1).start()
            copy(way, 0).start()

    def middle():
        for way in (0, 1):
            block = own(place(way, 2))
            copy(way, 0).wait_recv()
            copy(way, 1).wait_recv()
            block = block + pair_r[way, 0].astype(F32)
            got = far_r[way].astype(F32)
            low, high = block[:, :cut], block[:, cut:]
            low, high = (low + got, high) if way == 0 else (low, high + got)
            near_s[way, :, :cut] = low.astype(BF)
            near_s[way, :, cut:] = high.astype(BF)
            copy(way, 2).start()

    def last():
        block = own(index) + pair_r[0, 1].astype(F32) + pair_r[1, 1].astype(F32)
        copy(0, 2).wait_recv()
        copy(1, 2).wait_recv()
        finish(block + near_r[0].astype(F32) + near_r[1].astype(F32))

    def drain():
        for way in (0, 1):
            for kind in range(3):
                copy(way, kind).wait_send()

    return [first, middle, last], drain


def ring_of_four(index, own, send, recv, ssem, rsem, devices, finish):
    def copy(n):
        return remote(send.at[n], recv.at[n], ssem.at[n], rsem.at[n], devices[n])

    def first():
        for n in (1, 0, 2):
            send[n] = own(lax.rem(index + n + 1, 4)).astype(BF)
            copy(n).start()

    def last():
        block = own(index)
        for n in range(3):
            copy(n).wait_recv()
            block = block + recv[n].astype(F32)
        finish(block)

    def drain():
        for n in range(3):
            copy(n).wait_send()

    return [first, last], drain


def play(streams):
    events = []
    for times, steps in streams:
        events += [(t, len(events) + n, step) for n, (t, step) in enumerate(zip(times, steps))]
    for _, _, step in sorted(events, key=lambda e: e[:2]):
        step()


def kernel(rows_total, rows_hbm, w_ref, table_ref, ids_ref, wg_hbm, rg_hbm, qg_hbm, s):
    hop = lax.axis_index("hop")
    place = lax.axis_index("batch")
    core = lax.rem(place, NC)
    x = lax.rem(place // NC, NX)
    z = lax.rem(place // (NC * NX), NZ)
    y = place // (NC * NX * NZ)

    def at(h, yy, zz, xx, cc):
        return (h, ((yy * NZ + zz) * NX + xx) * NC + cc)

    other_core = at(hop, y, z, x, 1 - core)
    other_hop = at(1 - hop, y, z, x, core)
    other_x = at(hop, y, z, 1 - x, core)
    diagonal = at(hop, y, z, 1 - x, 1 - core)
    across = at(1 - hop, y, z, 1 - x, core)
    y_ways = (at(hop, lax.rem(y + 1, NY), z, x, core), at(hop, lax.rem(y + NY - 1, NY), z, x, core))
    z_ways = (at(hop, y, lax.rem(z + 1, NZ), x, core), at(hop, y, lax.rem(z + NZ - 1, NZ), x, core))

    rows_ref, wg_ref, rg_ref = s.rows, s.wg, s.rg
    tokens, width = rows_ref.shape
    half = width // 2
    wide = half // CHUNKS
    rels = table_ref.shape[0]
    colour = width // 2
    piece = colour // PIECES
    group = NZ * (NY // 2) // CHUNKS

    def w_copy(j):
        part = pl.ds(j * wide, wide)
        return pltpu.make_async_copy(w_ref.at[part], s.w.at[part], s.w_sem.at[j])

    table_copy = pltpu.make_async_copy(table_ref, s.table, s.table_sem)
    rows_copy = pltpu.make_async_copy(rows_hbm, rows_ref, s.rows_sem)
    rows_copy.start()
    w_copy(0).start()
    w_copy(CHUNKS).start()

    y_far = at(hop, lax.rem(y + NY // 2, NY), z, x, core)
    z_two = (at(hop, y, lax.rem(z + 2, NZ), x, core), at(hop, y, lax.rem(z + NZ - 2, NZ), x, core))
    partners = (other_core, other_hop, other_x, diagonal, across, y_far) + y_ways + z_ways + z_two
    barrier = pltpu.get_barrier_semaphore()
    for device in partners:
        pl.semaphore_signal(barrier, inc=1, device_id=device, device_id_type=MESH)

    def lead(k):
        for part in range(2):
            w_copy(k + part * CHUNKS).wait()
            weight = s.w[pl.ds(part * half + k * wide, wide)]
            s.q_s[k, :, part * wide:(part + 1) * wide] = dot_t(rows_ref[...], weight).astype(BF)

    for k in range(1, CHUNKS):
        w_copy(k).start()
        w_copy(k + CHUNKS).start()
    table_copy.start()
    rows_copy.wait()
    pl.when(hop == 0)(lambda: lead(0))
    pl.semaphore_wait(barrier, len(partners))

    w, turned = s.w, s.turned

    def hop_copy(src, dst, b, k):
        line = pl.ds(STARTS[b], SIZES[b])
        return remote(
            getattr(s, src).at[k, line], getattr(s, dst).at[k, line], s.hop_sem.at[0, b, k], s.hop_sem.at[1, b, k], across
        )

    def line_of(b):
        return slice(STARTS[b], STARTS[b] + SIZES[b])

    def out_parts(src, k):
        return [
            pltpu.make_async_copy(
                getattr(s, src).at[k, :, pl.ds(part * wide, wide)],
                qg_hbm.at[:, pl.ds(part * half + k * wide, wide)],
                s.qg_sem.at[k, part],
            )
            for part in range(2)
        ]

    def write_grads():
        pairs = ((wg_ref, wg_hbm, 0), (rg_ref, rg_hbm, 1))
        copies = [pltpu.make_async_copy(src, dst, s.grad_sem.at[n]) for src, dst, n in pairs]
        for copy in copies:
            copy.start()
        for copy in copies:
            copy.wait()

    def q_copy(b, k):
        return hop_copy("q_s", "q_r", b, k)

    def g_copy(b, k):
        return hop_copy("g_s", "g_r", b, k)

    def spot(k):
        return k // (CHUNKS // 2), k % (CHUNKS // 2) * group

    def turn(k, re, im):
        low, z0 = spot(k)
        for part, values in enumerate((re, im)):
            flat = values.astype(F32).T.astype(BF)
            for g in range(group):
                for xx in range(NX):
                    for cc in range(NC):
                        row = ((g * NX + xx) * NC + cc) * 16
                        turned[part, low, z0 + g, xx, cc] = flat[row:row + 16]

    def bufs(name):
        return [getattr(s, name + "_" + b) for b in ("sf", "sn", "rf", "rn", "ss", "rs")]

    def sub(refs, p):
        return [r.at[p] for r in refs]

    def weight_rings(name, left, right, rows, streams, drains, end):
        depth = right.shape[0]

        def by_z(cols):
            def own(zz):
                a = left[:, :, zz].reshape(NY * rows, depth)
                return dot(a, right[:, cols])
            return own

        def by_y(cols):
            def own(yy):
                a = left[yy // 2, lax.rem(yy, 2)].reshape(NZ * rows, depth)
                return dot(a, right[:, cols])
            return own

        for p in range(PIECES):
            here = slice(p * piece, (p + 1) * piece)
            cols = (here, slice(colour + p * piece, colour + (p + 1) * piece))

            def keep_z(v, here=here):
                getattr(s, name + "_sum_z")[:, :, here] = v.reshape(NY, rows, piece)

            def keep_y(v, here=here):
                getattr(s, name + "_sum_y")[:, :, here] = v.reshape(NZ, rows, piece)

            def from_z(yy, here=here):
                return getattr(s, name + "_sum_z")[yy, :, here]

            def from_y(zz, here=here):
                return getattr(s, name + "_sum_y")[zz, :, here]

            last_z, more_z = end(p, 0, cols[0])
            last_y, more_y = end(p, 1, cols[1])
            one = ring(NZ, z, by_z(cols[0]), *sub(bufs(name + "_az"), p), z_ways, keep_z)
            direct = [getattr(s, name + "_ay_" + b).at[p] for b in ("sn", "rn", "ss", "rs")]
            two = ring_of_four(y, from_z, *direct, (y_ways[0], y_far, y_ways[1]), last_z)
            three = ring(NY, y, by_y(cols[1]), *sub(bufs(name + "_by"), p), y_ways, keep_y)
            refs = {b: getattr(s, name + "_bz_" + b).at[p] for b in ("sp", "sf", "sn", "rp", "rf", "rn", "ss", "rs")}
            four = ring_of_eight(
                z, from_y, [refs[b] for b in ("sp", "sf", "sn")], [refs[b] for b in ("rp", "rf", "rn")],
                refs["ss"], refs["rs"], z_ways, z_two, last_y,
            )
            streams.append(([t + 0.5 * p for t in Z_FIRST], one[0] + two[0] + more_z))
            streams.append(([t + 0.5 * p + 0.25 for t in Y_FIRST], three[0] + four[0] + more_y))
            drains += [one[1], two[1], three[1], four[1]]

    scale = 1.0 / math.sqrt(rows_total)
    rel_scale = math.sqrt(rels / rows_total)

    def rel_copy(src, slot, sem, device):
        return remote(s.rel_s.at[src], s.rel_r.at[slot], s.rel_sem.at[0, sem], s.rel_sem.at[1, sem], device)

    def rel_y_copy(n):
        target = lax.rem(y + n, NY)
        return remote(
            s.rel_o.at[target], s.rel_i.at[n - 1], s.rel_y_sem.at[0, n - 1], s.rel_y_sem.at[1, n - 1],
            (y_ways[0], y_far, y_ways[1])[n - 1],
        )

    def rel_tail(drains):
        def own(zz):
            return s.rp[zz]

        def split(v):
            for yy in range(NY):
                for side in range(2):
                    s.rel_o[yy, side:side + 1] = v[yy * 2 + side:yy * 2 + side + 1]
            for n in range(1, NY):
                rel_y_copy(n).start()

        def final():
            for n in range(1, NY):
                rel_y_copy(n).wait_recv()
            total = s.rel_o[y] + s.rel_i[0] + s.rel_i[1] + s.rel_i[2]
            rg_ref[:, :half] = total[0:1] * rel_scale
            rg_ref[:, half:] = total[1:2] * rel_scale

        steps, drain = ring(NZ, z, own, *bufs("rz"), z_ways, split)
        drains.append(drain)
        drains.append(lambda: [rel_y_copy(n).wait_send() for n in range(1, NY)])
        return steps + [final]

    @pl.when(hop == 0)
    def _():
        left, right = s.left0, s.right0
        dest = (None, other_core, other_x, diagonal)

        def slot(n):
            return right.at[pl.ds(n * tokens, tokens)]

        sends = s.right0_sem
        to_core = remote(rows_ref, slot(1), sends.at[0, 0], sends.at[1, 0], other_core)
        to_x = remote(rows_ref, slot(2), sends.at[0, 1], sends.at[1, 1], other_x)
        onward = remote(slot(2), slot(3), sends.at[0, 2], sends.at[1, 2], other_core)
        to_x.start()

        for k in range(CHUNKS):
            if k:
                lead(k)
            q_copy(0, k).start()
        for b in range(1, BLOCKS):
            for k in range(CHUNKS):
                q_copy(b, k).start()
        to_core.start()
        right[0:tokens] = rows_ref[...]
        table_copy.wait()

        def left_copy(k, n):
            low, z0 = spot(k)
            xx, cc = (x, 1 - core) if n == 1 else (1 - x, core if n == 2 else 1 - core)
            return remote(
                turned.at[:, low, pl.ds(z0, group), xx, cc],
                left.at[:, low, pl.ds(z0, group), :, pl.ds(n * tokens, tokens)],
                s.left0_sem.at[0, k, n - 1], s.left0_sem.at[1, k, n - 1], dest[n],
            )

        for b in range(BLOCKS):
            for k in range(CHUNKS):
                g_copy(b, k).wait_recv()
                if b == BLOCKS - 1:
                    low, z0 = spot(k)
                    turn(k, s.g_r[k, :, :wide], s.g_r[k, :, wide:])
                    for n in (2, 3, 1):
                        left_copy(k, n).start()
                    left[:, low, z0:z0 + group, :, 0:tokens] = turned[:, low, z0:z0 + group, x, core]
                    for copy in out_parts("g_r", k):
                        copy.start()
            if b == 0:
                to_x.wait_recv()
                onward.start()
        to_core.wait()
        to_x.wait_send()
        onward.wait()
        for k in range(CHUNKS):
            for n in (1, 2, 3):
                left_copy(k, n).wait()

        streams, drains = [], []

        def end(p, which, cols):
            def last(v):
                wg_ref[:, cols] = v * scale
            return last, []

        def rel_take():
            for slot in range(NX):
                rel_copy(0, slot, slot, across).wait_recv()
            s.rp[...] = s.rel_r[0].astype(F32) + s.rel_r[1].astype(F32)

        weight_rings("h0", left, right, 16, streams, drains, end)
        streams.append((RELATION[2:], [rel_take] + rel_tail(drains)))
        play(streams)
        write_grads()
        for k in range(CHUNKS):
            for b in range(BLOCKS):
                q_copy(b, k).wait_send()
            for copy in out_parts("g_r", k):
                copy.wait()
        for drain in drains:
            drain()

    @pl.when(hop == 1)
    def _():
        left, right = s.left1, s.right1

        def cot_copy(b):
            line = pl.ds(STARTS[b], SIZES[b])
            return remote(rows_ref.at[line], s.cot.at[line], s.cot_sem.at[0, b], s.cot_sem.at[1, b], other_x)

        def out_copy(k):
            return remote(s.g_s.at[k], s.o_r.at[k], s.out_sem.at[0, k], s.out_sem.at[1, k], other_x)

        def right_copy(b):
            return remote(
                right.at[pl.ds(STARTS[b], SIZES[b])], right.at[pl.ds(tokens + STARTS[b], SIZES[b])],
                s.right1_sem.at[0, b], s.right1_sem.at[1, b], other_core,
            )

        def left_copy(k):
            low, z0 = spot(k)
            return remote(
                turned.at[:, low, pl.ds(z0, group), :, 1 - core],
                left.at[:, low, pl.ds(z0, group), :, :, pl.ds(tokens, tokens)],
                s.left1_sem.at[0, k], s.left1_sem.at[1, k], other_core,
            )

        ids_copy = remote(ids_ref, s.ids, s.ids_sem.at[0], s.ids_sem.at[1], other_x)
        ids_copy.start()
        for b in range(BLOCKS):
            cot_copy(b).start()
        ids_copy.wait()
        ids = s.ids[...]
        rows_of = lax.broadcasted_iota(jnp.int32, (rels, tokens), 0)
        onehot = jnp.where(rows_of == ids, 1.0, 0.0).T.astype(BF)
        table_copy.wait()
        for n in range(CHUNKS):
            part = slice(n * 2 * wide, (n + 1) * 2 * wide)
            s.rel[:, part] = dot(onehot, s.table[:, part]).astype(BF)
        for k in range(CHUNKS):
            w_copy(k).wait()
            w_copy(k + CHUNKS).wait()

        def columns(k):
            return slice(k * wide, (k + 1) * wide), slice(half + k * wide, half + (k + 1) * wide)

        def forward(b, k):
            re, im = columns(k)
            line = line_of(b)
            r_re, r_im = s.rel[line, re].astype(F32), s.rel[line, im].astype(F32)
            q_copy(b, k).wait_recv()
            q_re = s.q_r[k, line, :wide].astype(F32)
            q_im = s.q_r[k, line, wide:].astype(F32)
            z_re = (q_re * r_re - q_im * r_im).astype(BF)
            z_im = (q_re * r_im + q_im * r_re).astype(BF)
            s.mixed[line, re] = z_re
            s.mixed[line, im] = z_im
            for n in range(CHUNKS):
                part = slice(n * 2 * wide, (n + 1) * 2 * wide)
                term = dot(z_re, w[re, part]) + dot(z_im, w[im, part])
                s.pre[line, part] = term if k == 0 else s.pre[line, part] + term

        def activate(b):
            line = line_of(b)
            cot_copy(b).wait_recv()
            for n in range(CHUNKS):
                part = slice(n * 2 * wide, (n + 1) * 2 * wide)
                pre = s.pre[line, part]
                sig = 1.0 / (1.0 + jnp.exp(-pre))
                slope = sig * (1.0 + pre * (1.0 - sig))
                right[line, part] = (s.cot[line, part].astype(F32) * slope).astype(BF)
            right_copy(b).start()

        def back(b, k):
            re, im = columns(k)
            line = line_of(b)
            g_a = right[line]
            gz_re = dot_t(g_a, w[re])
            gz_im = dot_t(g_a, w[im])
            r_re, r_im = s.rel[line, re].astype(F32), s.rel[line, im].astype(F32)
            s.g_s[k, line, :wide] = (gz_re * r_re + gz_im * r_im).astype(BF)
            s.g_s[k, line, wide:] = (gz_im * r_re - gz_re * r_im).astype(BF)
            g_copy(b, k).start()
            q_re = s.q_r[k, line, :wide].astype(F32)
            q_im = s.q_r[k, line, wide:].astype(F32)
            s.pre[line, re] = gz_re * q_re + gz_im * q_im
            s.pre[line, im] = gz_im * q_re - gz_re * q_im

        def share(k):
            re, im = columns(k)
            low, z0 = spot(k)
            turn(k, s.mixed[:, re], s.mixed[:, im])
            left_copy(k).start()
            left[:, low, z0:z0 + group, :, :, 0:tokens] = turned[:, low, z0:z0 + group, :, core]

        for b in range(BLOCKS):
            for k in range(CHUNKS):
                forward(b, k)
                if b == BLOCKS - 1:
                    share(k)
            activate(b)
            for k in range(CHUNKS):
                back(b, k)
        for b in range(BLOCKS):
            right_copy(b).wait()
        for k in range(CHUNKS):
            left_copy(k).wait()

        swap = remote(s.rp_s, s.rp_r, s.rel_sem.at[0, 3], s.rel_sem.at[1, 3], other_core)
        aims = ((0, x, other_hop), (1, 1 - x, across), (2, 1 - x, other_x))

        def rel_start():
            row = lax.broadcasted_iota(jnp.int32, (rels, tokens), 0)
            side_of = lax.rem(row, 2)
            yy, zz = lax.rem(row // 2, NY), lax.rem(row // (2 * NY), NZ)
            hx = row // (2 * NY * NZ)
            base = (hx // NX) * (rels // 2) + ((yy * NZ + zz) * NX + lax.rem(hx, NX)) * NC
            who = s.ids[...]

            def partial_for(which):
                match = jnp.where(base + which == who, 1.0, 0.0)
                total = None
                for side in range(2):
                    pick = jnp.where(side_of == side, match, 0.0).astype(BF)
                    values = s.pre[:, side * half:(side + 1) * half]
                    head = values.astype(BF)
                    tail = (values - head.astype(F32)).astype(BF)
                    term = dot(pick, head) + dot(pick, tail)
                    total = term if total is None else total + term
                return total.reshape(2 * NX, NZ, 2 * NY, half)

            s.rp_s[...] = partial_for(1 - core).astype(BF)
            swap.start()
            s.rp_o[...] = partial_for(core)

        def rel_send(n):
            if n == 0:
                return remote(s.rel_s.at[x], s.rel_r.at[x], s.rel_sem.at[0, 0], s.rel_sem.at[1, x], other_hop)
            if n == 1:
                return remote(s.rel_s.at[1 - x], s.rel_r.at[x], s.rel_sem.at[0, 1], s.rel_sem.at[1, x], across)
            return remote(s.rel_s.at[NX + 1 - x], s.rel_r.at[0], s.rel_sem.at[0, 2], s.rel_sem.at[1, 2], other_x)

        def rel_join():
            swap.wait()
            for n in range(2 * NX):
                s.rel_s[n] = (s.rp_o[n] + s.rp_r[n].astype(F32)).astype(BF)
            s.rp[...] = s.rp_o[NX + x] + s.rp_r[NX + x].astype(F32)
            for n in range(3):
                rel_send(n).start()
            for k in range(CHUNKS):
                out_copy(k).start()

        def rel_take():
            rel_send(2).wait_recv()
            s.rp[...] = s.rp[...] + s.rel_r[0].astype(F32)

        def x_copy(p, which):
            return remote(
                s.x_s.at[which, p], s.x_r.at[which, p],
                s.x_sem.at[0, which, p], s.x_sem.at[1, which, p], other_x,
            )

        def end(p, which, cols):
            def last(v):
                s.total[which, p] = v.reshape(NX, 16, piece)
                s.x_s[which, p] = s.total[which, p, 1 - x].astype(BF)
                x_copy(p, which).start()

            def more():
                x_copy(p, which).wait_recv()
                wg_ref[:, cols] = (s.total[which, p, x] + s.x_r[which, p].astype(F32)) * scale

            return last, [more]

        streams, drains = [], []
        weight_rings("h1", left, right, NX * 16, streams, drains, end)
        streams.append((RELATION, [rel_start, rel_join, rel_take] + rel_tail(drains)))
        def settle_query():
            for k in range(CHUNKS):
                out_copy(k).wait_recv()
                for copy in out_parts("o_r", k):
                    copy.start()

        streams.append(((29.5,), [settle_query]))
        play(streams)
        write_grads()
        for b in range(BLOCKS):
            cot_copy(b).wait_send()
            for k in range(CHUNKS):
                g_copy(b, k).wait_send()
        for k in range(CHUNKS):
            out_copy(k).wait_send()
            for copy in out_parts("o_r", k):
                copy.wait()
        for drain in drains:
            drain()
        for n in range(3):
            rel_send(n).wait_send()
        for which in range(2):
            for p in range(PIECES):
                x_copy(p, which).wait_send()


def settle(wg_in, rg_in, qg_in, wg_out, rg_out, qg_out):
    wg_out[0] = wg_in[...]
    rg_out[...] = rg_in[...]
    qg_out[...] = qg_in[...]


def local(section_rows, weights, relation_table, relation_ids):
    tokens, width = section_rows.shape[1:]
    rels = relation_table.shape[0]
    total = tokens * lax.axis_size("batch")
    half = width // 2
    wide = half // CHUNKS
    piece = width // 2 // PIECES
    V = pltpu.VMEM
    D = pltpu.SemaphoreType.DMA
    chunks = (CHUNKS, tokens, 2 * wide)

    scratch = dict(
        w=V((width, width), BF),
        rows=V((tokens, width), BF),
        wg=V((16, width), F32),
        rg=V((1, width), F32),
        table=V((rels, width), BF),
        w_sem=D((2 * CHUNKS,)),
        table_sem=D,
        hop_sem=D((2, BLOCKS, CHUNKS)),
        out_sem=D((2, CHUNKS)),
        qg_sem=D((CHUNKS, 2)),
        grad_sem=D((2,)),
        rows_sem=D,
        cot_sem=D((2, BLOCKS)),
        ids_sem=D((2,)),
        right0_sem=D((2, 3)),
        right1_sem=D((2, BLOCKS)),
        left0_sem=D((2, CHUNKS, 3)),
        left1_sem=D((2, CHUNKS)),
        rel_sem=D((2, 4)),
        x_sem=D((2, 2, PIECES)),
        q_s=V(chunks, BF),
        q_r=V(chunks, BF),
        g_s=V(chunks, BF),
        g_r=V(chunks, BF),
        o_r=V(chunks, BF),
        cot=V((tokens, width), BF),
        ids=V((1, tokens), jnp.int32),
        rel=V((tokens, width), BF),
        mixed=V((tokens, width), BF),
        pre=V((tokens, width), F32),
        turned=V((2, NY // 2, NZ, NX, NC, 16, tokens), BF),
        left0=V((2, NY // 2, NZ, 16, 4 * tokens), BF),
        right0=V((4 * tokens, width), BF),
        left1=V((2, NY // 2, NZ, NX, 16, 2 * tokens), BF),
        right1=V((2 * tokens, width), BF),
        rp=V((NZ, 2 * NY, half), F32),
        rp_o=V((2 * NX, NZ, 2 * NY, half), F32),
        rp_s=V((2 * NX, NZ, 2 * NY, half), BF),
        rp_r=V((2 * NX, NZ, 2 * NY, half), BF),
        rel_s=V((2 * NX, NZ, 2 * NY, half), BF),
        rel_r=V((NX, NZ, 2 * NY, half), BF),
        rel_o=V((NY, 2, half), F32),
        rel_i=V((NY - 1, 2, half), F32),
        rel_y_sem=D((2, NY - 1)),
        total=V((2, PIECES, NX, 16, piece), F32),
        x_s=V((2, PIECES, 16, piece), BF),
        x_r=V((2, PIECES, 16, piece), BF),
    )

    def ring_bufs(name, lead, n, rows, cols):
        h = n // 2
        for side in "sr":
            scratch[name + "_" + side + "f"] = V(lead + (2, rows, cols // 2), BF)
            scratch[name + "_" + side + "n"] = V(lead + (2, h - 1, rows, cols), BF)
            scratch[name + "_" + side + "s"] = D(lead + (2, h))

    for name, rows in (("h0", 16), ("h1", NX * 16)):
        ring_bufs(name + "_az", (PIECES,), NZ, NY * rows, piece)
        for side in "sr":
            scratch[name + "_ay_" + side + "n"] = V((PIECES, NY - 1, rows, piece), BF)
            scratch[name + "_ay_" + side + "s"] = D((PIECES, NY - 1))
        ring_bufs(name + "_by", (PIECES,), NY, NZ * rows, piece)
        for side in "sr":
            scratch[name + "_bz_" + side + "p"] = V((PIECES, 2, 2, rows, piece), BF)
            scratch[name + "_bz_" + side + "f"] = V((PIECES, 2, rows, piece // 2), BF)
            scratch[name + "_bz_" + side + "n"] = V((PIECES, 2, rows, piece), BF)
            scratch[name + "_bz_" + side + "s"] = D((PIECES, 2, 3))
        scratch[name + "_sum_z"] = V((NY, rows, half), F32)
        scratch[name + "_sum_y"] = V((NZ, rows, half), F32)
    ring_bufs("rz", (), NZ, 2 * NY, half)
    names = list(scratch)

    def body(*refs):
        kernel(total, *refs[:7], types.SimpleNamespace(**dict(zip(names, refs[7:]))))

    vmem = pl.BlockSpec(memory_space=pltpu.VMEM)
    hbm = pl.BlockSpec(memory_space=pl.ANY)
    wg, rg, qg = pl.pallas_call(
        body,
        out_shape=(
            jax.ShapeDtypeStruct((16, width), F32),
            jax.ShapeDtypeStruct((1, width), F32),
            jax.ShapeDtypeStruct((tokens, width), BF),
        ),
        in_specs=[hbm, hbm, hbm, vmem],
        out_specs=(hbm, hbm, hbm),
        scratch_shapes=[scratch[n] for n in names],
        compiler_params=pltpu.CompilerParams(
            collective_id=0, has_side_effects=True, vmem_limit_bytes=60 * 1024 * 1024
        ),
        name="backward",
    )(section_rows[0], weights[0], relation_table, relation_ids.reshape(1, tokens))
    shapes = (
        jax.ShapeDtypeStruct((1, 16, width), F32),
        jax.ShapeDtypeStruct((1, width), F32),
        jax.ShapeDtypeStruct((tokens, width), BF),
    )
    return pl.pallas_call(
        settle, out_shape=shapes, in_specs=[vmem] * 3, out_specs=(vmem, vmem, vmem), name="settle"
    )(wg, rg, qg)


def solution(mesh):
    return jax.shard_map(
        local,
        mesh=mesh,
        in_specs=(P("hop", "batch", None), P("hop", None, None), P(), P("batch")),
        out_specs=(P("hop", "batch", None), P(("hop", "batch"), None), P("batch", None)),
        check_vma=False,
    )
```

```python
import functools
import math
import types

import jax
import jax.numpy as jnp
from jax import lax
from jax.experimental import pallas as pl
from jax.experimental.pallas import tpu as pltpu
from jax.sharding import PartitionSpec as P

MESH = pl.DeviceIdType.MESH
BF = jnp.bfloat16
F32 = jnp.float32
NY, NZ, NX, NC = 4, 8, 2, 2
CHUNKS = 4
PIECES = 2
SIZES = (64, 64)
BLOCKS = len(SIZES)
STARTS = tuple(sum(SIZES[:n]) for n in range(BLOCKS))
Z_FIRST = (0, 4, 10, 16, 22, 22.5, 26.5, 30)
Y_FIRST = (0, 7, 19, 19.5, 23.4, 27.5, 31)
RELATION = (1.5, 5.5, 14.5, 14.6, 18.1, 21.1, 24.1, 27.1, 31.1)


def dot(a, b):
    return jnp.dot(a, b, preferred_element_type=F32)


def dot_t(a, b):
    return lax.dot_general(a, b, (((1,), (1,)), ((), ())), preferred_element_type=F32)


def remote(src, dst, send, recv, device):
    return pltpu.make_async_remote_copy(
        src_ref=src, dst_ref=dst, send_sem=send, recv_sem=recv,
        device_id=device, device_id_type=MESH,
    )


def ring(n, index, own, send_far, send_near, recv_far, recv_near, ssem, rsem, devices, finish):
    half = n // 2
    cut = send_far.shape[-1]

    def copy(way, step):
        src = send_far.at[way] if step == 1 else send_near.at[way, step - 2]
        dst = recv_far.at[way] if step == 1 else recv_near.at[way, step - 2]
        return remote(src, dst, ssem.at[way, step - 1], rsem.at[way, step - 1], devices[way])

    def first():
        block = own(lax.rem(index + half, n)).astype(BF)
        send_far[0] = block[:, :cut]
        copy(0, 1).start()
        send_far[1] = block[:, cut:]
        copy(1, 1).start()

    def middle(step):
        distance = half + 1 - step
        for way in (0, 1):
            target = lax.rem(index + (distance if way == 0 else n - distance), n)
            block = own(target)
            copy(way, step - 1).wait_recv()
            if step == 2:
                got = recv_far[way].astype(F32)
                low, high = block[:, :cut], block[:, cut:]
                low, high = (low + got, high) if way == 0 else (low, high + got)
                send_near[way, 0, :, :cut] = low.astype(BF)
                send_near[way, 0, :, cut:] = high.astype(BF)
            else:
                got = recv_near[way, step - 3].astype(F32)
                send_near[way, step - 2] = (block + got).astype(BF)
            copy(way, step).start()

    def last():
        block = own(index)
        copy(0, half).wait_recv()
        copy(1, half).wait_recv()
        finish(block + recv_near[0, half - 2].astype(F32) + recv_near[1, half - 2].astype(F32))

    def drain():
        for step in range(1, half + 1):
            for way in (0, 1):
                copy(way, step).wait_send()

    return [first] + [functools.partial(middle, t) for t in range(2, half + 1)] + [last], drain


def ring_of_eight(index, own, sends, recvs, ssem, rsem, one_away, two_away, finish):
    n = 8
    pair_s, far_s, near_s = sends
    pair_r, far_r, near_r = recvs
    cut = far_s.shape[-1]

    def copy(way, kind):
        src, dst = ((pair_s, pair_r), (far_s, far_r), (near_s, near_r))[kind]
        device = (one_away if kind == 0 else two_away)[way]
        return remote(src.at[way], dst.at[way], ssem.at[way, kind], rsem.at[way, kind], device)

    def place(way, distance):
        return lax.rem(index + (distance if way == 0 else n - distance), n)

    def first():
        block = own(lax.rem(index + 4, n)).astype(BF)
        for way in (0, 1):
            pair_s[way, 0] = own(place(way, 3)).astype(BF)
            pair_s[way, 1] = own(place(way, 1)).astype(BF)
            far_s[way] = block[:, :cut] if way == 0 else block[:, cut:]
            copy(way, 1).start()
            copy(way, 0).start()

    def middle():
        for way in (0, 1):
            block = own(place(way, 2))
            copy(way, 0).wait_recv()
            copy(way, 1).wait_recv()
            block = block + pair_r[way, 0].astype(F32)
            got = far_r[way].astype(F32)
            low, high = block[:, :cut], block[:, cut:]
            low, high = (low + got, high) if way == 0 else (low, high + got)
            near_s[way, :, :cut] = low.astype(BF)
            near_s[way, :, cut:] = high.astype(BF)
            copy(way, 2).start()

    def last():
        block = own(index) + pair_r[0, 1].astype(F32) + pair_r[1, 1].astype(F32)
        copy(0, 2).wait_recv()
        copy(1, 2).wait_recv()
        finish(block + near_r[0].astype(F32) + near_r[1].astype(F32))

    def drain():
        for way in (0, 1):
            for kind in range(3):
                copy(way, kind).wait_send()

    return [first, middle, last], drain


def ring_of_four(index, own, send, recv, ssem, rsem, devices, finish):
    def copy(n):
        return remote(send.at[n], recv.at[n], ssem.at[n], rsem.at[n], devices[n])

    def first():
        for n in (1, 0, 2):
            send[n] = own(lax.rem(index + n + 1, 4)).astype(BF)
            copy(n).start()

    def last():
        block = own(index)
        for n in range(3):
            copy(n).wait_recv()
            block = block + recv[n].astype(F32)
        finish(block)

    def drain():
        for n in range(3):
            copy(n).wait_send()

    return [first, last], drain


def play(streams):
    events = []
    for times, steps in streams:
        events += [(t, len(events) + n, step) for n, (t, step) in enumerate(zip(times, steps))]
    for _, _, step in sorted(events, key=lambda e: e[:2]):
        step()


def kernel(rows_total, rows_hbm, w_ref, table_ref, ids_ref, wg_hbm, rg_hbm, qg_hbm, s):
    hop = lax.axis_index("hop")
    place = lax.axis_index("batch")
    core = lax.rem(place, NC)
    x = lax.rem(place // NC, NX)
    z = lax.rem(place // (NC * NX), NZ)
    y = place // (NC * NX * NZ)

    def at(h, yy, zz, xx, cc):
        return (h, ((yy * NZ + zz) * NX + xx) * NC + cc)

    other_core = at(hop, y, z, x, 1 - core)
    other_hop = at(1 - hop, y, z, x, core)
    other_x = at(hop, y, z, 1 - x, core)
    diagonal = at(hop, y, z, 1 - x, 1 - core)
    across = at(1 - hop, y, z, 1 - x, core)
    y_ways = (at(hop, lax.rem(y + 1, NY), z, x, core), at(hop, lax.rem(y + NY - 1, NY), z, x, core))
    z_ways = (at(hop, y, lax.rem(z + 1, NZ), x, core), at(hop, y, lax.rem(z + NZ - 1, NZ), x, core))

    rows_ref, wg_ref, rg_ref = s.rows, s.wg, s.rg
    tokens, width = rows_ref.shape
    half = width // 2
    wide = half // CHUNKS
    rels = table_ref.shape[0]
    colour = width // 2
    piece = colour // PIECES
    group = NZ * (NY // 2) // CHUNKS

    def w_copy(j):
        part = pl.ds(j * wide, wide)
        return pltpu.make_async_copy(w_ref.at[part], s.w.at[part], s.w_sem.at[j])

    table_copy = pltpu.make_async_copy(table_ref, s.table, s.table_sem)
    rows_copy = pltpu.make_async_copy(rows_hbm, rows_ref, s.rows_sem)
    rows_copy.start()
    w_copy(0).start()
    w_copy(CHUNKS).start()

    y_far = at(hop, lax.rem(y + NY // 2, NY), z, x, core)
    z_two = (at(hop, y, lax.rem(z + 2, NZ), x, core), at(hop, y, lax.rem(z + NZ - 2, NZ), x, core))
    partners = (other_core, other_hop, other_x, diagonal, across, y_far) + y_ways + z_ways + z_two
    barrier = pltpu.get_barrier_semaphore()
    for device in partners:
        pl.semaphore_signal(barrier, inc=1, device_id=device, device_id_type=MESH)

    def lead(k):
        for part in range(2):
            w_copy(k + part * CHUNKS).wait()
            weight = s.w[pl.ds(part * half + k * wide, wide)]
            s.q_s[k, :, part * wide:(part + 1) * wide] = dot_t(rows_ref[...], weight).astype(BF)

    for k in range(1, CHUNKS):
        w_copy(k).start()
        w_copy(k + CHUNKS).start()
    table_copy.start()
    rows_copy.wait()
    pl.when(hop == 0)(lambda: lead(0))
    pl.semaphore_wait(barrier, len(partners))

    w, turned = s.w, s.turned

    def hop_copy(src, dst, b, k):
        line = pl.ds(STARTS[b], SIZES[b])
        return remote(
            getattr(s, src).at[k, line], getattr(s, dst).at[k, line], s.hop_sem.at[0, b, k], s.hop_sem.at[1, b, k], across
        )

    def line_of(b):
        return slice(STARTS[b], STARTS[b] + SIZES[b])

    def out_parts(src, k):
        return [
            pltpu.make_async_copy(
                getattr(s, src).at[k, :, pl.ds(part * wide, wide)],
                qg_hbm.at[:, pl.ds(part * half + k * wide, wide)],
                s.qg_sem.at[k, part],
            )
            for part in range(2)
        ]

    def write_grads():
        pairs = ((wg_ref, wg_hbm, 0), (rg_ref, rg_hbm, 1))
        copies = [pltpu.make_async_copy(src, dst, s.grad_sem.at[n]) for src, dst, n in pairs]
        for copy in copies:
            copy.start()
        for copy in copies:
            copy.wait()

    def q_copy(b, k):
        return hop_copy("q_s", "q_r", b, k)

    def g_copy(b, k):
        return hop_copy("g_s", "g_r", b, k)

    def spot(k):
        return k // (CHUNKS // 2), k % (CHUNKS // 2) * group

    def turn(k, re, im):
        low, z0 = spot(k)
        for part, values in enumerate((re, im)):
            flat = values.astype(F32).T.astype(BF)
            for g in range(group):
                for xx in range(NX):
                    for cc in range(NC):
                        row = ((g * NX + xx) * NC + cc) * 16
                        turned[part, low, z0 + g, xx, cc] = flat[row:row + 16]

    def bufs(name):
        return [getattr(s, name + "_" + b) for b in ("sf", "sn", "rf", "rn", "ss", "rs")]

    def sub(refs, p):
        return [r.at[p] for r in refs]

    def weight_rings(name, left, right, rows, streams, drains, end):
        depth = right.shape[0]

        def by_z(cols):
            def own(zz):
                a = left[:, :, zz].reshape(NY * rows, depth)
                return dot(a, right[:, cols])
            return own

        def by_y(cols):
            def own(yy):
                a = left[yy // 2, lax.rem(yy, 2)].reshape(NZ * rows, depth)
                return dot(a, right[:, cols])
            return own

        for p in range(PIECES):
            here = slice(p * piece, (p + 1) * piece)
            cols = (here, slice(colour + p * piece, colour + (p + 1) * piece))

            def keep_z(v, here=here):
                getattr(s, name + "_sum_z")[:, :, here] = v.reshape(NY, rows, piece)

            def keep_y(v, here=here):
                getattr(s, name + "_sum_y")[:, :, here] = v.reshape(NZ, rows, piece)

            def from_z(yy, here=here):
                return getattr(s, name + "_sum_z")[yy, :, here]

            def from_y(zz, here=here):
                return getattr(s, name + "_sum_y")[zz, :, here]

            last_z, more_z = end(p, 0, cols[0])
            last_y, more_y = end(p, 1, cols[1])
            one = ring(NZ, z, by_z(cols[0]), *sub(bufs(name + "_az"), p), z_ways, keep_z)
            direct = [getattr(s, name + "_ay_" + b).at[p] for b in ("sn", "rn", "ss", "rs")]
            two = ring_of_four(y, from_z, *direct, (y_ways[0], y_far, y_ways[1]), last_z)
            three = ring(NY, y, by_y(cols[1]), *sub(bufs(name + "_by"), p), y_ways, keep_y)
            refs = {b: getattr(s, name + "_bz_" + b).at[p] for b in ("sp", "sf", "sn", "rp", "rf", "rn", "ss", "rs")}
            four = ring_of_eight(
                z, from_y, [refs[b] for b in ("sp", "sf", "sn")], [refs[b] for b in ("rp", "rf", "rn")],
                refs["ss"], refs["rs"], z_ways, z_two, last_y,
            )
            streams.append(([t + 0.5 * p for t in Z_FIRST], one[0] + two[0] + more_z))
            streams.append(([t + 0.5 * p + 0.25 for t in Y_FIRST], three[0] + four[0] + more_y))
            drains += [one[1], two[1], three[1], four[1]]

    scale = 1.0 / math.sqrt(rows_total)
    rel_scale = math.sqrt(rels / rows_total)

    def rel_copy(src, slot, sem, device):
        return remote(s.rel_s.at[src], s.rel_r.at[slot], s.rel_sem.at[0, sem], s.rel_sem.at[1, sem], device)

    def rel_y_copy(n):
        target = lax.rem(y + n, NY)
        return remote(
            s.rel_o.at[target], s.rel_i.at[n - 1], s.rel_y_sem.at[0, n - 1], s.rel_y_sem.at[1, n - 1],
            (y_ways[0], y_far, y_ways[1])[n - 1],
        )

    def rel_tail(drains):
        def own(zz):
            return s.rp[zz]

        def split(v):
            for yy in range(NY):
                for side in range(2):
                    s.rel_o[yy, side:side + 1] = v[yy * 2 + side:yy * 2 + side + 1]
            for n in range(1, NY):
                rel_y_copy(n).start()

        def final():
            for n in range(1, NY):
                rel_y_copy(n).wait_recv()
            total = s.rel_o[y] + s.rel_i[0] + s.rel_i[1] + s.rel_i[2]
            rg_ref[:, :half] = total[0:1] * rel_scale
            rg_ref[:, half:] = total[1:2] * rel_scale

        steps, drain = ring(NZ, z, own, *bufs("rz"), z_ways, split)
        drains.append(drain)
        drains.append(lambda: [rel_y_copy(n).wait_send() for n in range(1, NY)])
        return steps + [final]

    @pl.when(hop == 0)
    def _():
        left, right = s.left0, s.right0
        dest = (None, other_core, other_x, diagonal)

        def slot(n):
            return right.at[pl.ds(n * tokens, tokens)]

        sends = s.right0_sem
        to_core = remote(rows_ref, slot(1), sends.at[0, 0], sends.at[1, 0], other_core)
        to_x = remote(rows_ref, slot(2), sends.at[0, 1], sends.at[1, 1], other_x)
        onward = remote(slot(2), slot(3), sends.at[0, 2], sends.at[1, 2], other_core)
        to_x.start()

        for k in range(CHUNKS):
            if k:
                lead(k)
            q_copy(0, k).start()
        for b in range(1, BLOCKS):
            for k in range(CHUNKS):
                q_copy(b, k).start()
        to_core.start()
        right[0:tokens] = rows_ref[...]
        table_copy.wait()

        def left_copy(k, n):
            low, z0 = spot(k)
            xx, cc = (x, 1 - core) if n == 1 else (1 - x, core if n == 2 else 1 - core)
            return remote(
                turned.at[:, low, pl.ds(z0, group), xx, cc],
                left.at[:, low, pl.ds(z0, group), :, pl.ds(n * tokens, tokens)],
                s.left0_sem.at[0, k, n - 1], s.left0_sem.at[1, k, n - 1], dest[n],
            )

        for b in range(BLOCKS):
            for k in range(CHUNKS):
                g_copy(b, k).wait_recv()
                if b == BLOCKS - 1:
                    low, z0 = spot(k)
                    turn(k, s.g_r[k, :, :wide], s.g_r[k, :, wide:])
                    for n in (2, 3, 1):
                        left_copy(k, n).start()
                    left[:, low, z0:z0 + group, :, 0:tokens] = turned[:, low, z0:z0 + group, x, core]
                    for copy in out_parts("g_r", k):
                        copy.start()
            if b == 0:
                to_x.wait_recv()
                onward.start()
        to_core.wait()
        to_x.wait_send()
        onward.wait()
        for k in range(CHUNKS):
            for n in (1, 2, 3):
                left_copy(k, n).wait()

        streams, drains = [], []

        def end(p, which, cols):
            def last(v):
                wg_ref[:, cols] = v * scale
            return last, []

        def rel_take():
            for slot in range(NX):
                rel_copy(0, slot, slot, across).wait_recv()
            s.rp[...] = s.rel_r[0].astype(F32) + s.rel_r[1].astype(F32)

        weight_rings("h0", left, right, 16, streams, drains, end)
        streams.append((RELATION[2:], [rel_take] + rel_tail(drains)))
        play(streams)
        write_grads()
        for k in range(CHUNKS):
            for b in range(BLOCKS):
                q_copy(b, k).wait_send()
            for copy in out_parts("g_r", k):
                copy.wait()
        for drain in drains:
            drain()

    @pl.when(hop == 1)
    def _():
        left, right = s.left1, s.right1

        def cot_copy(b):
            line = pl.ds(STARTS[b], SIZES[b])
            return remote(rows_ref.at[line], s.cot.at[line], s.cot_sem.at[0, b], s.cot_sem.at[1, b], other_x)

        def out_copy(k):
            return remote(s.g_s.at[k], s.o_r.at[k], s.out_sem.at[0, k], s.out_sem.at[1, k], other_x)

        def right_copy(b):
            return remote(
                right.at[pl.ds(STARTS[b], SIZES[b])], right.at[pl.ds(tokens + STARTS[b], SIZES[b])],
                s.right1_sem.at[0, b], s.right1_sem.at[1, b], other_core,
            )

        def left_copy(k):
            low, z0 = spot(k)
            return remote(
                turned.at[:, low, pl.ds(z0, group), :, 1 - core],
                left.at[:, low, pl.ds(z0, group), :, :, pl.ds(tokens, tokens)],
                s.left1_sem.at[0, k], s.left1_sem.at[1, k], other_core,
            )

        ids_copy = remote(ids_ref, s.ids, s.ids_sem.at[0], s.ids_sem.at[1], other_x)
        ids_copy.start()
        for b in range(BLOCKS):
            cot_copy(b).start()
        ids_copy.wait()
        ids = s.ids[...]
        rows_of = lax.broadcasted_iota(jnp.int32, (rels, tokens), 0)
        onehot = jnp.where(rows_of == ids, 1.0, 0.0).T.astype(BF)
        table_copy.wait()
        for n in range(CHUNKS):
            part = slice(n * 2 * wide, (n + 1) * 2 * wide)
            s.rel[:, part] = dot(onehot, s.table[:, part]).astype(BF)
        for k in range(CHUNKS):
            w_copy(k).wait()
            w_copy(k + CHUNKS).wait()

        def columns(k):
            return slice(k * wide, (k + 1) * wide), slice(half + k * wide, half + (k + 1) * wide)

        def forward(b, k):
            re, im = columns(k)
            line = line_of(b)
            r_re, r_im = s.rel[line, re].astype(F32), s.rel[line, im].astype(F32)
            q_copy(b, k).wait_recv()
            q_re = s.q_r[k, line, :wide].astype(F32)
            q_im = s.q_r[k, line, wide:].astype(F32)
            z_re = (q_re * r_re - q_im * r_im).astype(BF)
            z_im = (q_re * r_im + q_im * r_re).astype(BF)
            s.mixed[line, re] = z_re
            s.mixed[line, im] = z_im
            for n in range(CHUNKS):
                part = slice(n * 2 * wide, (n + 1) * 2 * wide)
                term = dot(z_re, w[re, part]) + dot(z_im, w[im, part])
                s.pre[line, part] = term if k == 0 else s.pre[line, part] + term

        def activate(b):
            line = line_of(b)
            cot_copy(b).wait_recv()
            for n in range(CHUNKS):
                part = slice(n * 2 * wide, (n + 1) * 2 * wide)
                pre = s.pre[line, part]
                sig = 1.0 / (1.0 + jnp.exp(-pre))
                slope = sig * (1.0 + pre * (1.0 - sig))
                right[line, part] = (s.cot[line, part].astype(F32) * slope).astype(BF)
            right_copy(b).start()

        def back(b, k):
            re, im = columns(k)
            line = line_of(b)
            g_a = right[line]
            gz_re = dot_t(g_a, w[re])
            gz_im = dot_t(g_a, w[im])
            r_re, r_im = s.rel[line, re].astype(F32), s.rel[line, im].astype(F32)
            s.g_s[k, line, :wide] = (gz_re * r_re + gz_im * r_im).astype(BF)
            s.g_s[k, line, wide:] = (gz_im * r_re - gz_re * r_im).astype(BF)
            g_copy(b, k).start()
            q_re = s.q_r[k, line, :wide].astype(F32)
            q_im = s.q_r[k, line, wide:].astype(F32)
            s.pre[line, re] = gz_re * q_re + gz_im * q_im
            s.pre[line, im] = gz_im * q_re - gz_re * q_im

        def share(k):
            re, im = columns(k)
            low, z0 = spot(k)
            turn(k, s.mixed[:, re], s.mixed[:, im])
            left_copy(k).start()
            left[:, low, z0:z0 + group, :, :, 0:tokens] = turned[:, low, z0:z0 + group, :, core]

        for b in range(BLOCKS):
            for k in range(CHUNKS):
                forward(b, k)
                if b == BLOCKS - 1:
                    share(k)
            activate(b)
            for k in range(CHUNKS):
                back(b, k)
        for b in range(BLOCKS):
            right_copy(b).wait()
        for k in range(CHUNKS):
            left_copy(k).wait()

        swap = remote(s.rp_s, s.rp_r, s.rel_sem.at[0, 3], s.rel_sem.at[1, 3], other_core)
        aims = ((0, x, other_hop), (1, 1 - x, across), (2, 1 - x, other_x))

        def rel_start():
            row = lax.broadcasted_iota(jnp.int32, (rels, tokens), 0)
            side_of = lax.rem(row, 2)
            yy, zz = lax.rem(row // 2, NY), lax.rem(row // (2 * NY), NZ)
            hx = row // (2 * NY * NZ)
            base = (hx // NX) * (rels // 2) + ((yy * NZ + zz) * NX + lax.rem(hx, NX)) * NC
            who = s.ids[...]

            def partial_for(which):
                match = jnp.where(base + which == who, 1.0, 0.0)
                total = None
                for side in range(2):
                    pick = jnp.where(side_of == side, match, 0.0).astype(BF)
                    values = s.pre[:, side * half:(side + 1) * half]
                    head = values.astype(BF)
                    tail = (values - head.astype(F32)).astype(BF)
                    term = dot(pick, head) + dot(pick, tail)
                    total = term if total is None else total + term
                return total.reshape(2 * NX, NZ, 2 * NY, half)

            s.rp_s[...] = partial_for(1 - core).astype(BF)
            swap.start()
            s.rp_o[...] = partial_for(core)

        def rel_send(n):
            if n == 0:
                return remote(s.rel_s.at[x], s.rel_r.at[x], s.rel_sem.at[0, 0], s.rel_sem.at[1, x], other_hop)
            if n == 1:
                return remote(s.rel_s.at[1 - x], s.rel_r.at[x], s.rel_sem.at[0, 1], s.rel_sem.at[1, x], across)
            return remote(s.rel_s.at[NX + 1 - x], s.rel_r.at[0], s.rel_sem.at[0, 2], s.rel_sem.at[1, 2], other_x)

        def rel_join():
            swap.wait()
            for n in range(2 * NX):
                s.rel_s[n] = (s.rp_o[n] + s.rp_r[n].astype(F32)).astype(BF)
            s.rp[...] = s.rp_o[NX + x] + s.rp_r[NX + x].astype(F32)
            for n in range(3):
                rel_send(n).start()
            for k in range(CHUNKS):
                out_copy(k).start()

        def rel_take():
            rel_send(2).wait_recv()
            s.rp[...] = s.rp[...] + s.rel_r[0].astype(F32)

        def x_copy(p, which):
            return remote(
                s.x_s.at[which, p], s.x_r.at[which, p],
                s.x_sem.at[0, which, p], s.x_sem.at[1, which, p], other_x,
            )

        def end(p, which, cols):
            def last(v):
                s.total[which, p] = v.reshape(NX, 16, piece)
                s.x_s[which, p] = s.total[which, p, 1 - x].astype(BF)
                x_copy(p, which).start()

            def more():
                x_copy(p, which).wait_recv()
                wg_ref[:, cols] = (s.total[which, p, x] + s.x_r[which, p].astype(F32)) * scale

            return last, [more]

        streams, drains = [], []
        weight_rings("h1", left, right, NX * 16, streams, drains, end)
        streams.append((RELATION, [rel_start, rel_join, rel_take] + rel_tail(drains)))
        def settle_query():
            for k in range(CHUNKS):
                out_copy(k).wait_recv()
                for copy in out_parts("o_r", k):
                    copy.start()

        streams.append(((29.5,), [settle_query]))
        play(streams)
        write_grads()
        for b in range(BLOCKS):
            cot_copy(b).wait_send()
            for k in range(CHUNKS):
                g_copy(b, k).wait_send()
        for k in range(CHUNKS):
            out_copy(k).wait_send()
            for copy in out_parts("o_r", k):
                copy.wait()
        for drain in drains:
            drain()
        for n in range(3):
            rel_send(n).wait_send()
        for which in range(2):
            for p in range(PIECES):
                x_copy(p, which).wait_send()


def settle(wg_in, rg_in, qg_in, wg_out, rg_out, qg_out, sems):
    pairs = ((qg_in, qg_out), (wg_in, wg_out.at[0]), (rg_in, rg_out))
    copies = [pltpu.make_async_copy(src, dst, sems.at[n]) for n, (src, dst) in enumerate(pairs)]
    for copy in copies:
        copy.start()
    for copy in copies:
        copy.wait()


def local(section_rows, weights, relation_table, relation_ids):
    tokens, width = section_rows.shape[1:]
    rels = relation_table.shape[0]
    total = tokens * lax.axis_size("batch")
    half = width // 2
    wide = half // CHUNKS
    piece = width // 2 // PIECES
    V = pltpu.VMEM
    D = pltpu.SemaphoreType.DMA
    chunks = (CHUNKS, tokens, 2 * wide)

    scratch = dict(
        w=V((width, width), BF),
        rows=V((tokens, width), BF),
        wg=V((16, width), F32),
        rg=V((1, width), F32),
        table=V((rels, width), BF),
        w_sem=D((2 * CHUNKS,)),
        table_sem=D,
        hop_sem=D((2, BLOCKS, CHUNKS)),
        out_sem=D((2, CHUNKS)),
        qg_sem=D((CHUNKS, 2)),
        grad_sem=D((2,)),
        rows_sem=D,
        cot_sem=D((2, BLOCKS)),
        ids_sem=D((2,)),
        right0_sem=D((2, 3)),
        right1_sem=D((2, BLOCKS)),
        left0_sem=D((2, CHUNKS, 3)),
        left1_sem=D((2, CHUNKS)),
        rel_sem=D((2, 4)),
        x_sem=D((2, 2, PIECES)),
        q_s=V(chunks, BF),
        q_r=V(chunks, BF),
        g_s=V(chunks, BF),
        g_r=V(chunks, BF),
        o_r=V(chunks, BF),
        cot=V((tokens, width), BF),
        ids=V((1, tokens), jnp.int32),
        rel=V((tokens, width), BF),
        mixed=V((tokens, width), BF),
        pre=V((tokens, width), F32),
        turned=V((2, NY // 2, NZ, NX, NC, 16, tokens), BF),
        left0=V((2, NY // 2, NZ, 16, 4 * tokens), BF),
        right0=V((4 * tokens, width), BF),
        left1=V((2, NY // 2, NZ, NX, 16, 2 * tokens), BF),
        right1=V((2 * tokens, width), BF),
        rp=V((NZ, 2 * NY, half), F32),
        rp_o=V((2 * NX, NZ, 2 * NY, half), F32),
        rp_s=V((2 * NX, NZ, 2 * NY, half), BF),
        rp_r=V((2 * NX, NZ, 2 * NY, half), BF),
        rel_s=V((2 * NX, NZ, 2 * NY, half), BF),
        rel_r=V((NX, NZ, 2 * NY, half), BF),
        rel_o=V((NY, 2, half), F32),
        rel_i=V((NY - 1, 2, half), F32),
        rel_y_sem=D((2, NY - 1)),
        total=V((2, PIECES, NX, 16, piece), F32),
        x_s=V((2, PIECES, 16, piece), BF),
        x_r=V((2, PIECES, 16, piece), BF),
    )

    def ring_bufs(name, lead, n, rows, cols):
        h = n // 2
        for side in "sr":
            scratch[name + "_" + side + "f"] = V(lead + (2, rows, cols // 2), BF)
            scratch[name + "_" + side + "n"] = V(lead + (2, h - 1, rows, cols), BF)
            scratch[name + "_" + side + "s"] = D(lead + (2, h))

    for name, rows in (("h0", 16), ("h1", NX * 16)):
        ring_bufs(name + "_az", (PIECES,), NZ, NY * rows, piece)
        for side in "sr":
            scratch[name + "_ay_" + side + "n"] = V((PIECES, NY - 1, rows, piece), BF)
            scratch[name + "_ay_" + side + "s"] = D((PIECES, NY - 1))
        ring_bufs(name + "_by", (PIECES,), NY, NZ * rows, piece)
        for side in "sr":
            scratch[name + "_bz_" + side + "p"] = V((PIECES, 2, 2, rows, piece), BF)
            scratch[name + "_bz_" + side + "f"] = V((PIECES, 2, rows, piece // 2), BF)
            scratch[name + "_bz_" + side + "n"] = V((PIECES, 2, rows, piece), BF)
            scratch[name + "_bz_" + side + "s"] = D((PIECES, 2, 3))
        scratch[name + "_sum_z"] = V((NY, rows, half), F32)
        scratch[name + "_sum_y"] = V((NZ, rows, half), F32)
    ring_bufs("rz", (), NZ, 2 * NY, half)
    names = list(scratch)

    def body(*refs):
        kernel(total, *refs[:7], types.SimpleNamespace(**dict(zip(names, refs[7:]))))

    vmem = pl.BlockSpec(memory_space=pltpu.VMEM)
    hbm = pl.BlockSpec(memory_space=pl.ANY)
    wg, rg, qg = pl.pallas_call(
        body,
        out_shape=(
            jax.ShapeDtypeStruct((16, width), F32),
            jax.ShapeDtypeStruct((1, width), F32),
            jax.ShapeDtypeStruct((tokens, width), BF),
        ),
        in_specs=[hbm, hbm, hbm, vmem],
        out_specs=(hbm, hbm, hbm),
        scratch_shapes=[scratch[n] for n in names],
        compiler_params=pltpu.CompilerParams(
            collective_id=0, has_side_effects=True, vmem_limit_bytes=60 * 1024 * 1024
        ),
        name="backward",
    )(section_rows[0], weights[0], relation_table, relation_ids.reshape(1, tokens))
    shapes = (
        jax.ShapeDtypeStruct((1, 16, width), F32),
        jax.ShapeDtypeStruct((1, width), F32),
        jax.ShapeDtypeStruct((tokens, width), BF),
    )
    return pl.pallas_call(
        settle, out_shape=shapes, in_specs=[hbm] * 3, out_specs=(vmem, vmem, vmem),
        scratch_shapes=[D((3,))], name="settle",
    )(wg, rg, qg)


def solution(mesh):
    return jax.shard_map(
        local,
        mesh=mesh,
        in_specs=(P("hop", "batch", None), P("hop", None, None), P(), P("batch")),
        out_specs=(P("hop", "batch", None), P(("hop", "batch"), None), P("batch", None)),
        check_vma=False,
    )
```
